32 devices in a mesh: wide: 16 (over z, x, core), narrow: 2 (over y).
Axes of the slice: x: 2, y: 2, z: 4, core: 2. Of those that a mesh axis runs over, the one named last changes fastest.
Arguments:
- tokens: bfloat16 [16384, 1152], P(('wide', 'narrow')), may hold values from -6 to 6
- conditions: bfloat16 [64, 1152], P('wide'), may hold values from -6 to 6
- segment_ids: int32 [16384], P(('wide', 'narrow')), may hold values from 0 to 3, as said below
- pad_mask: int32 [16384], P(('wide', 'narrow')), may hold values from 0 to 1, as said below
- segment_image: int32 [16, 4], P('wide'), may hold values from 0 to 3, each once within a row
- ada_weight: bfloat16 [1152, 6912], P(None, 'narrow'), may hold values from -0.1875 to 0.1875
- ada_bias: bfloat16 [6912], P('narrow'), may hold values from -3 to 3
- qkv_weight: bfloat16 [1152, 3456], replicated, may hold values from -0.1875 to 0.1875
- trunk_bias: bfloat16 [9216], replicated, may hold values from -2 to 2
- proj_weight: bfloat16 [1152, 1152], replicated, may hold values from -0.75 to 0.75
- fc1_weight: bfloat16 [1152, 4608], replicated, may hold values from -0.1875 to 0.1875
- fc2_weight: bfloat16 [4608, 1152], replicated, may hold values from -0.09375 to 0.09375
- output_grad: bfloat16 [16384, 1152], P(('wide', 'narrow')), may hold values from -6 to 6
Outputs:
- output: bfloat16 [16384, 1152], P(('wide', 'narrow'))
- tokens_grad: float32 [16384, 1152], P(('wide', 'narrow'))
- conditions_grad: float32 [64, 1152], P('wide', 'narrow')
- ada_weight_grad: float32 [1152, 6912], P(None, 'narrow')
- ada_bias_grad: float32 [6912], P('narrow')
- qkv_grad: float32 [2, 1990656], P('narrow', 'wide')
- bias_grad: float32 [9216], P(('wide', 'narrow'))
- proj_grad: float32 [2, 663552], P('narrow', 'wide')
- fc1_grad: float32 [2, 2654208], P('narrow', 'wide')
- fc2_grad: float32 [2, 2654208], P('narrow', 'wide')
The draws below stay inside these ranges and needn't reach their ends.
Inputs may be any that keep to these rules, and one draw needn't show every extreme that they name: `segment_ids`: within each group of 1024 tokens the ids start at 0 and rise by one from image to image; every image is 1024 or 256 tokens long and starts at a multiple of its length. `pad_mask`: in each image the padded tokens, if any, follow the real ones; an image's first token is real. `segment_image`: each row is a permutation.
All inputs are finite; a program needn't handle non-finite values.
Results may differ from the reference program's by a relative error of at most 0.02.
Values may be sent and summed in bfloat16 or wider, within the bound.
No kernel may reach another device: no remote copies, remote signals or barrier semaphores. Data moves between devices by JAX's collectives and lax.ppermute only.
A program may use at most 384 MiB of HBM per device.

```python
import jax
import jax.numpy as jnp
from jax import lax

D = 1152
HEADS = 16
HEAD = 72
FF = 4608
BIG = 1024
SMALL = 256
GROUP = 1024
GROUPS = 16
NSEG = 4
CONDS = 64
TOKENS = 16384
N_NARROW = 2


def packing(key):
    block_count = GROUP // BIG
    ratio = BIG // SMALL
    kinds = jax.random.randint(jax.random.fold_in(key, 7), (GROUPS, block_count), 0, 2)
    group_index = jnp.arange(GROUPS, dtype=jnp.int32)[:, None]
    kinds = jnp.where(group_index == 0, 0, jnp.where(group_index == 1, 1, kinds))
    per_block = jnp.where(kinds == 1, 1, ratio)
    first_id = jnp.cumsum(per_block, axis=1) - per_block
    places = jnp.arange(GROUP, dtype=jnp.int32)
    block_of = places // BIG
    offset = places % BIG
    big_token = kinds[:, block_of]
    piece = jnp.where(big_token == 1, 0, offset // SMALL)
    segment = first_id[:, block_of] + piece
    length = jnp.where(big_token == 1, BIG, SMALL)
    inside = jnp.where(big_token == 1, offset, offset % SMALL)
    pad_big = jax.random.randint(jax.random.fold_in(key, 8), (GROUPS, block_count), 0, BIG // 4 + 1)
    pad_small = jax.random.randint(jax.random.fold_in(key, 9), (GROUPS, block_count, ratio), 0, SMALL // 4 + 1)
    small_cut = jnp.take_along_axis(pad_small[:, block_of, :], piece[:, :, None], axis=2)[:, :, 0]
    cut = jnp.where(big_token == 1, pad_big[:, block_of], small_cut)
    valid = (inside < length - cut).astype(jnp.int32)
    return (segment.reshape(-1).astype(jnp.int32), valid.reshape(-1))


def draw_segment_ids(key, part):
    return packing(key)[0]


def draw_pad_mask(key, part):
    return packing(key)[1]


def steps_of(stream_key, dims, pieces, smallest, high):
    gain, own = 1.0, jax.random.fold_in(stream_key, 6)
    for position, blocks in pieces:
        steps = jnp.exp(jax.random.uniform(jax.random.fold_in(own, position), (blocks,), jnp.float32, smallest / len(pieces), high / len(pieces)))
        gain = gain * jnp.repeat(steps, dims[position] // blocks).reshape([-1 if axis == position else 1 for axis in range(len(dims))])
    return gain


def gaussian(rng, shape, width, reach, cuts=(), kind=jnp.bfloat16):
    factor_of = steps_of(rng, shape, cuts, -0.22, 0.18) if cuts else 1.0
    array = jax.random.normal(rng, shape, jnp.float32) * width * factor_of
    return jnp.minimum(jnp.maximum(array, -reach), reach).astype(kind)


def setup_inputs(seed: int = 0) -> dict:
    streams_of = jax.random.split(jax.random.key(seed), 14)
    return {
        "tokens": gaussian(streams_of[0], (TOKENS, D), 1.0, 6.0, ((0, 32),)),
        "conditions": gaussian(streams_of[1], (CONDS, D), 1.0, 6.0, ((0, 16),)),
        "segment_ids": draw_segment_ids(jax.random.fold_in(streams_of[13], 71), 0),
        "pad_mask": draw_pad_mask(jax.random.fold_in(streams_of[13], 71), 0),
        "segment_image": jax.vmap(lambda own: jax.random.permutation(own, NSEG))(jax.random.split(streams_of[4], GROUPS)).reshape((GROUPS, NSEG)).astype(jnp.int32),
        "ada_weight": gaussian(streams_of[5], (D, 6 * D), D ** -0.5, 0.1875, ((1, 2),)),
        "ada_bias": gaussian(streams_of[6], (6 * D,), 0.5, 3.0, ((0, 2),)),
        "qkv_weight": gaussian(streams_of[7], (D, 3 * D), D ** -0.5, 0.1875),
        "trunk_bias": gaussian(streams_of[8], (4 * D + FF,), 0.3, 2.0),
        "proj_weight": gaussian(streams_of[9], (D, D), (D // 16) ** -0.5, 0.75),
        "fc1_weight": gaussian(streams_of[10], (D, FF), D ** -0.5, 0.1875),
        "fc2_weight": gaussian(streams_of[11], (FF, D), FF ** -0.5, 0.09375),
        "output_grad": gaussian(streams_of[12], (TOKENS, D), 1.0, 6.0, ((0, 32),)),
    }


HIGHEST = lax.Precision.HIGHEST
EPSILON = 1e-06
MASKED = -1e+30

@jax.custom_vjp
def low(v):
    return lax.optimization_barrier(v.astype(jnp.bfloat16)).astype(jnp.float32)

@jax.custom_vjp
def low_back(v):
    return v

def low_keep(v):
    return (low(v), None)

def low_pass(kept, grad):
    return (grad,)

def back_keep(v):
    return (v, None)

def back_low(kept, grad):
    return (low(grad),)
low.defvjp(low_keep, low_pass)
low_back.defvjp(back_keep, back_low)

def layer_norm(values):
    centred = values - lax.optimization_barrier(jnp.mean(values, axis=-1, keepdims=True))
    variance = lax.optimization_barrier(jnp.mean(centred * centred, axis=-1, keepdims=True))
    return centred * lax.rsqrt(variance + EPSILON)

def attend(queries, keys, values, segment, valid):
    count = queries.shape[0]
    block_rows = min(512, count)
    block_count = count // block_rows
    factor = HEAD ** (-0.5)
    key_heads = keys.reshape(count, HEADS, HEAD)
    value_heads = values.reshape(count, HEADS, HEAD)
    places = jnp.arange(count, dtype=jnp.int32)

    def one_block(query_block, segment_block, place_block):
        scores = jnp.einsum('qhd,khd->qhk', query_block, key_heads, precision=HIGHEST) * factor
        scores = low_back(scores)
        allowed = (segment_block[:, None] == segment[None, :]) & ((valid[None, :] == 1) | (place_block[:, None] == places[None, :]))
        scores = jnp.where(allowed[:, None, :], scores, MASKED)
        highest = lax.optimization_barrier(jnp.max(scores, axis=-1, keepdims=True))
        weights = jnp.exp(scores - highest)
        probs = low(weights / lax.optimization_barrier(jnp.sum(weights, axis=-1, keepdims=True)))
        return jnp.einsum('qhk,khd->qhd', probs, value_heads, precision=HIGHEST)
    checked = jax.checkpoint(one_block)

    def mapped(block_item):
        return checked(block_item[0], block_item[1], block_item[2])
    results = lax.map(mapped, (queries.reshape(block_count, block_rows, HEADS, HEAD), segment.reshape(block_count, block_rows), places.reshape(block_count, block_rows)))
    return results.reshape(count, HEADS * HEAD)

def block_layer(tokens, conditions, weights, segment, valid, images):
    ada_weight, ada_bias, qkv_weight, trunk_bias, proj_weight, fc1_weight, fc2_weight = weights
    model_width = tokens.shape[1]
    hidden_width = fc1_weight.shape[1]
    act = low(jax.nn.silu(conditions))
    modulation = low(low_back(jnp.dot(act, ada_weight, precision=HIGHEST) + ada_bias))
    per_token = modulation[images[segment]]
    shift_one, scale_one, gate_one, shift_two, scale_two, gate_two = jnp.split(per_token, 6, axis=1)
    first_in = low(layer_norm(tokens) * (1.0 + scale_one) + shift_one)
    projected = jnp.dot(first_in, qkv_weight, precision=HIGHEST)
    query_bias = trunk_bias[:model_width]
    value_bias = trunk_bias[model_width:2 * model_width]
    proj_bias = trunk_bias[2 * model_width:3 * model_width]
    first_bias = trunk_bias[3 * model_width:3 * model_width + hidden_width]
    second_bias = trunk_bias[3 * model_width + hidden_width:]
    queries = low(low_back(projected[:, :model_width] + query_bias))
    keys = low(low_back(projected[:, model_width:2 * model_width]))
    values = low(low_back(projected[:, 2 * model_width:] + value_bias))
    attended = low(low_back(attend(queries, keys, values, segment, valid)))
    branch_one = low_back(jnp.dot(attended, proj_weight, precision=HIGHEST) + proj_bias)
    middle = tokens + gate_one * branch_one
    second_in = low(layer_norm(middle) * (1.0 + scale_two) + shift_two)
    before = low_back(jnp.dot(second_in, fc1_weight, precision=HIGHEST) + first_bias)
    hidden = low(jax.nn.gelu(before, approximate=True))
    branch_two = low_back(jnp.dot(hidden, fc2_weight, precision=HIGHEST) + second_bias)
    return middle + gate_two * branch_two

def column_blocks(matrix):
    row_total, column_total = matrix.shape
    return matrix.reshape(row_total, N_NARROW, column_total // N_NARROW).transpose(1, 0, 2).reshape(N_NARROW, -1)

def reference(tokens, conditions, segment_ids, pad_mask, segment_image, ada_weight, ada_bias, qkv_weight, trunk_bias, proj_weight, fc1_weight, fc2_weight, output_grad):
    weights = tuple((w.astype(jnp.float32) for w in (ada_weight, ada_bias, qkv_weight, trunk_bias, proj_weight, fc1_weight, fc2_weight)))
    inputs = (tokens.astype(jnp.float32).reshape(GROUPS, GROUP, D), conditions.astype(jnp.float32).reshape(GROUPS, NSEG, D), segment_ids.reshape(GROUPS, GROUP), pad_mask.reshape(GROUPS, GROUP), segment_image, output_grad.astype(jnp.float32).reshape(GROUPS, GROUP, D))

    def per_group(totals, group_item):
        group_tokens, group_conditions, segment, valid, images, cotangent = group_item

        def run(tokens_in, conditions_in, ada_w, ada_b, qkv_w, bias_all, proj_w, fc1_w, fc2_w):
            return block_layer(tokens_in, conditions_in, (ada_w, ada_b, qkv_w, bias_all, proj_w, fc1_w, fc2_w), segment, valid, images)
        result, pullback = jax.vjp(run, group_tokens, group_conditions, *weights)
        grads = pullback(cotangent)
        totals = tuple((total + grad for total, grad in zip(totals, grads[2:])))
        return (totals, (result.astype(jnp.bfloat16), grads[0], grads[1]))
    start = tuple((jnp.zeros(w.shape, jnp.float32) for w in weights))
    totals, (results, token_grads, condition_grads) = lax.scan(per_group, start, inputs)
    return (results.reshape(TOKENS, D), token_grads.reshape(TOKENS, D), condition_grads.reshape(CONDS, D), totals[0], totals[1], column_blocks(totals[2]), totals[3], column_blocks(totals[4]), column_blocks(totals[5]), column_blocks(totals[6]))
```

```python
import functools
import math

import jax
import jax.numpy as jnp
from jax import lax
from jax.experimental import pallas as pl
from jax.experimental.pallas import tpu as pltpu
from jax.sharding import PartitionSpec as P

HEADS = 16
HEAD = 72
BIG = 1024
SMALL = 256
EPSILON = 1e-06
MASKED = -1e30
FACTOR = HEAD ** (-0.5)
LOG2E = math.log2(math.e)
BF16 = jnp.bfloat16
F32 = jnp.float32


def swap(x, axis, size, mask):
    return lax.ppermute(x, axis, [(i, i ^ mask) for i in range(size)])


def gather_relative(x, axis, size):
    out = x[None]
    mask = 1
    while mask < size:
        out = jnp.concatenate([out, swap(out, axis, size, mask)], axis=0)
        mask *= 2
    return out


def scatter_relative(mine, others, axis, size):
    total = mine.astype(F32)
    for j in range(1, size):
        total = total + swap(others[j - 1].astype(BF16), axis, size, j).astype(F32)
    return total


def absolute(blocks, me, size):
    if size == 2:
        return jnp.where(me == 0, blocks, blocks[::-1])
    return jnp.take(blocks, jnp.arange(size) ^ me, axis=0)


def halve(y, place, bit, axis, size, index, kind):
    mine = (index >> bit) & 1
    keep = lax.dynamic_index_in_dim(y, mine, place, keepdims=False)
    send = lax.dynamic_index_in_dim(y, 1 - mine, place, keepdims=False)
    got = swap(send.astype(kind), axis, size, 1 << bit)
    return (keep.astype(F32) + got.astype(F32)).astype(kind)


def halve_all(y, count, axis, size, index, kind):
    y = y.reshape((2,) * count + (y.shape[0] >> count,) + y.shape[1:])
    for bit in range(count):
        y = halve(y, count - 1 - bit, bit, axis, size, index, kind)
    return y


def rows_to_columns(y, n_wide, n_narrow, hi):
    repeat = n_wide // n_narrow
    width = y.shape[1] // n_narrow
    blocks = jnp.stack([y[:, i * width : (i + 1) * width] for i in range(n_narrow)])
    total = None
    for k in range(n_narrow):
        pairs = []
        for h in range(n_narrow):
            for j in range(repeat):
                for n in range(n_narrow):
                    source = (h * repeat + j) * n_narrow + n
                    target = (n * repeat + j) * n_narrow + (h + k) % n_narrow
                    pairs.append((source, target))
        send = lax.dynamic_index_in_dim(blocks, (hi + k) % n_narrow, 0, keepdims=False)
        got = lax.ppermute(send, ("wide", "narrow"), pairs).astype(F32)
        total = got if total is None else total + got
    return total


TILE = 256


def fill_mask(row_ref, col_ref, mask_ref):
    col = col_ref[0]
    row = row_ref[0]
    shape = (BIG, BIG)
    same = (col >> 1) == (row >> 1)
    own = lax.broadcasted_iota(jnp.int32, shape, 0) == lax.broadcasted_iota(jnp.int32, shape, 1)
    usable = jnp.broadcast_to((col & 1) == 1, shape) | own
    mask_ref[...] = jnp.where(same & usable, 0.0, MASKED)


def nn(a, b):
    return lax.dot_general(a, b, (((1,), (0,)), ((), ())), preferred_element_type=F32)


def nt(a, b):
    return lax.dot_general(a, b, (((1,), (1,)), ((), ())), preferred_element_type=F32)


def tn(a, b):
    return lax.dot_general(a, b, (((0,), (0,)), ((), ())), preferred_element_type=F32)


def forward_kernel(q_ref, k_ref, v_ref, row_ref, col_ref, o_ref, l_ref, mask_ref):
    @pl.when(pl.program_id(1) == 0)
    def _():
        fill_mask(row_ref, col_ref, mask_ref)

    keys = k_ref[0, 0].T
    values = v_ref[0, 0]
    for start in range(0, BIG, TILE):
        part = slice(start, start + TILE)
        scores = nn(keys, q_ref[0, 0, :, part]) * (FACTOR * LOG2E) + mask_ref[:, part]
        top = jnp.max(scores, axis=0, keepdims=True)
        weights = jnp.exp2(scores - top)
        total = jnp.sum(weights, axis=0, keepdims=True)
        mixed = nn(values, weights.astype(BF16))
        o_ref[0, :, part] = mixed / total
        l_ref[0, :, part] = top + jnp.log2(total)


def backward_kernel(
    q_ref, k_ref, v_ref, g_ref, o_ref, l_ref, row_ref, col_ref, d_ref, mask_ref
):
    @pl.when(pl.program_id(1) == 0)
    def _():
        fill_mask(row_ref, col_ref, mask_ref)

    keys_t = k_ref[0, 0]
    keys = keys_t.T
    values = v_ref[0, 0].T
    key_grad = jnp.zeros((BIG, HEAD), F32)
    value_grad = jnp.zeros((BIG, HEAD), F32)
    for start in range(0, BIG, TILE):
        part = slice(start, start + TILE)
        queries = q_ref[0, 0, :, part]
        grads = g_ref[0, :, part]
        delta = jnp.sum(grads.astype(F32) * o_ref[0, :, part], axis=0, keepdims=True)
        scores = nn(keys, queries) * (FACTOR * LOG2E) + mask_ref[:, part]
        probs = jnp.exp2(scores - l_ref[0, :, part])
        score_grad = (probs * (nn(values, grads) - delta)).astype(BF16)
        value_grad = value_grad + nt(probs.astype(BF16), grads)
        key_grad = key_grad + nt(score_grad, queries)
        d_ref[0, 0, :, part] = (nn(keys_t, score_grad) * FACTOR).astype(BF16)
    d_ref[1, 0] = (key_grad * FACTOR).T.astype(BF16)
    d_ref[2, 0] = value_grad.T.astype(BF16)


def projected_spec(kind):
    return pl.BlockSpec((1, 1, HEAD, BIG), lambda c, h: (kind, h, 0, c))


LABEL_SPECS = [
    pl.BlockSpec((1, 1, BIG), lambda c, h: (c, 0, 0)),
    pl.BlockSpec((1, BIG, 1), lambda c, h: (c, 0, 0)),
]
WIDE_SPEC = pl.BlockSpec((1, HEAD, BIG), lambda c, h: (h, 0, c))
LINE_SPEC = pl.BlockSpec((1, 1, BIG), lambda c, h: (h, 0, c))


def attend_forward(projected, labels):
    _, heads, _, count = projected.shape
    chunks = count // BIG
    return pl.pallas_call(
        forward_kernel,
        grid=(chunks, heads),
        in_specs=[projected_spec(0), projected_spec(1), projected_spec(2)] + LABEL_SPECS,
        out_specs=[WIDE_SPEC, LINE_SPEC],
        out_shape=[
            jax.ShapeDtypeStruct((heads, HEAD, count), F32),
            jax.ShapeDtypeStruct((heads, 1, count), F32),
        ],
        scratch_shapes=[pltpu.VMEM((BIG, BIG), F32)],
        name="attend_forward",
    )(
        projected,
        projected,
        projected,
        labels.reshape(chunks, 1, BIG),
        labels.reshape(chunks, BIG, 1),
    )


def attend_backward(projected, grads, attended, log_total, labels):
    _, heads, _, count = projected.shape
    chunks = count // BIG
    return pl.pallas_call(
        backward_kernel,
        grid=(chunks, heads),
        in_specs=[projected_spec(0), projected_spec(1), projected_spec(2)]
        + [WIDE_SPEC, WIDE_SPEC, LINE_SPEC]
        + LABEL_SPECS,
        out_specs=pl.BlockSpec((3, 1, HEAD, BIG), lambda c, h: (0, h, 0, c)),
        out_shape=jax.ShapeDtypeStruct((3, heads, HEAD, count), BF16),
        scratch_shapes=[pltpu.VMEM((BIG, BIG), F32)],
        name="attend_backward",
    )(
        projected,
        projected,
        projected,
        grads,
        attended,
        log_total,
        labels.reshape(chunks, 1, BIG),
        labels.reshape(chunks, BIG, 1),
    )


def normalise(values):
    centred = values - jnp.mean(values, axis=-1, keepdims=True)
    scale = lax.rsqrt(jnp.mean(centred * centred, axis=-1, keepdims=True) + EPSILON)
    return centred * scale, scale


def normalise_back(normed, scale, grad):
    return scale * (
        grad
        - jnp.mean(grad, axis=-1, keepdims=True)
        - normed * jnp.mean(grad * normed, axis=-1, keepdims=True)
    )


def blocked(x):
    return x.reshape(x.shape[0] // SMALL, SMALL, x.shape[1])


def flat(x):
    return x.reshape(x.shape[0] * x.shape[1], x.shape[2])


def body(
    n_wide,
    n_narrow,
    tokens,
    conditions,
    segment_ids,
    pad_mask,
    segment_image,
    ada_weight,
    ada_bias,
    qkv_weight,
    trunk_bias,
    proj_weight,
    fc1_weight,
    fc2_weight,
    output_grad,
):
    rows, width = tokens.shape
    hidden_width = fc1_weight.shape[1]
    me = lax.axis_index("narrow")
    wide = lax.axis_index("wide")
    stages = n_wide.bit_length() - 1
    low_stages = (n_wide // n_narrow).bit_length() - 1
    heads = HEADS // n_narrow
    head_width = heads * HEAD
    fc_width = hidden_width // n_narrow
    biases = trunk_bias.astype(F32)
    query_bias = biases[:width]
    value_bias = biases[width : 2 * width]
    proj_bias = biases[2 * width : 3 * width]
    first_bias = biases[3 * width : 3 * width + hidden_width]
    second_bias = biases[3 * width + hidden_width :]
    mine_of = functools.partial(lax.dynamic_slice_in_dim, axis=0)

    tokens_all = gather_relative(tokens, "narrow", n_narrow).reshape(-1, width)
    labels = gather_relative(segment_ids * 2 + pad_mask, "narrow", n_narrow).reshape(-1)
    output_grad_all = gather_relative(output_grad, "narrow", n_narrow).reshape(-1, width)

    conditions32 = conditions.astype(F32)
    act = jax.nn.silu(conditions32).astype(BF16)
    columns = (
        jnp.dot(act, ada_weight, preferred_element_type=F32) + ada_bias.astype(F32)
    ).astype(BF16)
    modulation = absolute(gather_relative(columns, "narrow", n_narrow), me, n_narrow)
    modulation = modulation.transpose(1, 0, 2).reshape(conditions.shape[0], -1)
    slots = labels[::SMALL] >> 1
    image_count = conditions.shape[0]
    image = jnp.sum(
        jnp.where(
            slots[:, None] == jnp.arange(image_count, dtype=jnp.int32)[None, :],
            segment_image[0][None, :],
            0,
        ),
        axis=1,
    )
    pick = image[:, None] == jnp.arange(image_count, dtype=jnp.int32)[None, :]
    per_block = jnp.dot(pick.astype(BF16), modulation, preferred_element_type=F32)
    pieces = [p[:, None, :] for p in jnp.split(per_block, 6, axis=1)]
    own_blocks = rows // SMALL
    shift1, scale1, gate1, shift2, scale2, gate2 = pieces
    own = [p[:own_blocks] for p in pieces]

    act_all = gather_relative(act, "wide", n_wide).reshape(-1, width)

    normed1_all, _ = normalise(tokens_all.astype(F32))
    first_in_all = flat(blocked(normed1_all) * (1.0 + scale1) + shift1).astype(BF16)
    qkv_mine = lax.dynamic_slice_in_dim(
        qkv_weight.reshape(width, 3, width), me * head_width, head_width, axis=2
    ).reshape(width, 3 * head_width)
    qkv_bias = jnp.concatenate(
        [
            mine_of(query_bias, me * head_width, head_width),
            jnp.zeros((head_width,), F32),
            mine_of(value_bias, me * head_width, head_width),
        ]
    )
    projected = (
        lax.dot_general(
            qkv_mine, first_in_all, (((0,), (1,)), ((), ())), preferred_element_type=F32
        )
        + qkv_bias[:, None]
    ).astype(BF16)
    projected = projected.reshape(3, heads, HEAD, -1)
    attended32, log_total = attend_forward(projected, labels)
    attended = attended32.reshape(head_width, -1).astype(BF16)
    shares = [attended[:, :rows]] + [
        swap(attended[:, j * rows : (j + 1) * rows], "narrow", n_narrow, j)
        for j in range(1, n_narrow)
    ]
    attended_own = absolute(jnp.stack(shares), me, n_narrow).reshape(width, rows)
    branch1 = tn(attended_own, proj_weight) + proj_bias
    tokens32 = tokens.astype(F32)
    middle = tokens32 + flat(own[2] * blocked(branch1))
    normed2, ratio2 = normalise(middle)
    second_in = flat(blocked(normed2) * (1.0 + own[4]) + own[3]).astype(BF16)

    second_in_all = gather_relative(second_in, "narrow", n_narrow).reshape(-1, width)
    fc1_mine = lax.dynamic_slice_in_dim(fc1_weight, me * fc_width, fc_width, axis=1)
    fc2_mine = lax.dynamic_slice_in_dim(fc2_weight, me * fc_width, fc_width, axis=0)
    branch2_grad_all = flat(gate2 * blocked(output_grad_all.astype(F32))).astype(BF16)
    hidden_grad = nt(branch2_grad_all, fc2_mine)
    before = nn(second_in_all, fc1_mine) + mine_of(first_bias, me * fc_width, fc_width)
    hidden, gelu_pull = jax.vjp(lambda v: jax.nn.gelu(v, approximate=True), before)
    hidden = hidden.astype(BF16)
    before_grad = gelu_pull(hidden_grad)[0].astype(BF16)
    second_in_part = nn_t(before_grad, fc1_mine)
    second_in_grad = reduce_tokens(second_in_part, rows, n_narrow)
    fc2_local = tn(hidden, branch2_grad_all).astype(BF16)
    fc1_local = tn(second_in_all, before_grad).astype(BF16)
    branch2_part = nn(hidden, fc2_mine)
    branch2 = reduce_tokens(branch2_part, rows, n_narrow) + second_bias
    output = (middle + flat(own[5] * blocked(branch2))).astype(BF16)

    fc2_sum = halve_all(fc2_local, low_stages, "wide", n_wide, wide, BF16)
    fc2_flat = rows_to_columns(fc2_sum, n_wide, n_narrow, wide >> low_stages)
    fc1_flat = halve_all(fc1_local, stages, "wide", n_wide, wide, BF16).astype(F32)

    output_grad32 = output_grad.astype(F32)
    gate2_terms = blocked(output_grad32 * branch2)
    scale2_terms = blocked(second_in_grad * normed2)
    middle_grad = output_grad32 + normalise_back(
        normed2, ratio2, flat(blocked(second_in_grad) * (1.0 + own[4]))
    )
    gate1_terms = blocked(middle_grad * branch1)
    branch1_grad = flat(own[2] * blocked(middle_grad)).astype(BF16)
    branch1_grad_all = gather_relative(branch1_grad, "narrow", n_narrow).reshape(-1, width)
    proj_mine = lax.dynamic_slice_in_dim(proj_weight, me * head_width, head_width, axis=0)
    attended_grad = nt(proj_mine, branch1_grad_all).astype(BF16).reshape(heads, HEAD, -1)
    projected_grad = attend_backward(projected, attended_grad, attended32, log_total, labels)
    projected_grad = projected_grad.reshape(3 * head_width, -1)
    proj_local = nn(attended, branch1_grad_all).astype(BF16)
    proj_sum = halve_all(proj_local, low_stages, "wide", n_wide, wide, BF16)
    proj_flat = rows_to_columns(proj_sum, n_wide, n_narrow, wide >> low_stages)

    qkv_local = lax.dot_general(
        first_in_all, projected_grad, (((0,), (1,)), ((), ())), preferred_element_type=F32
    ).astype(BF16)
    qkv_sum = halve_all(qkv_local, stages, "wide", n_wide, wide, BF16)
    qkv_all = absolute(gather_relative(qkv_sum, "narrow", n_narrow), me, n_narrow)
    qkv_all = qkv_all.reshape(n_narrow, qkv_sum.shape[0], 3, head_width)
    qkv_all = qkv_all.transpose(1, 2, 0, 3).reshape(qkv_sum.shape[0], 3 * width)
    qkv_block = 3 * width // n_narrow
    qkv_flat = lax.dynamic_slice_in_dim(qkv_all, me * qkv_block, qkv_block, axis=1)

    first_in_part = lax.dot_general(
        projected_grad, qkv_mine, (((0,), (1,)), ((), ())), preferred_element_type=F32
    )
    first_in_grad = reduce_tokens(first_in_part, rows, n_narrow)
    normed1, ratio1 = normalise(tokens32)
    scale1_terms = blocked(first_in_grad * normed1)
    tokens_grad = middle_grad + normalise_back(
        normed1, ratio1, flat(blocked(first_in_grad) * (1.0 + own[1]))
    )

    terms = [
        blocked(first_in_grad),
        scale1_terms,
        gate1_terms,
        blocked(second_in_grad),
        scale2_terms,
        gate2_terms,
    ]
    block_sums = jnp.concatenate([jnp.sum(t, axis=1) for t in terms], axis=1)
    modulation_part = jnp.dot(
        pick[:own_blocks].astype(F32).T, block_sums, precision=lax.Precision.HIGHEST
    )
    modulation_part = modulation_part.reshape(image_count, n_narrow, -1).transpose(1, 0, 2)
    relative = absolute(modulation_part, me, n_narrow)
    modulation_grad = scatter_relative(
        relative[0], [relative[j] for j in range(1, n_narrow)], "narrow", n_narrow
    ).astype(BF16)
    modulation_grad_all = gather_relative(modulation_grad, "wide", n_wide)
    modulation_grad_all = modulation_grad_all.reshape(-1, modulation_grad.shape[1])
    ada_weight_grad = tn(act_all, modulation_grad_all)
    ada_bias_grad = jnp.sum(modulation_grad_all.astype(F32), axis=0)
    act_part = nt(modulation_grad, ada_weight)
    act_part = act_part.reshape(image_count, n_narrow, -1).transpose(1, 0, 2)
    relative = absolute(act_part, me, n_narrow)
    act_grad = scatter_relative(
        relative[0], [relative[j] for j in range(1, n_narrow)], "narrow", n_narrow
    )
    column_width = width // n_narrow
    condition_mine = lax.dynamic_slice_in_dim(conditions32, me * column_width, column_width, 1)
    gate = 1.0 / (1.0 + jnp.exp(-condition_mine))
    conditions_grad = act_grad * (gate * (1.0 + condition_mine * (1.0 - gate)))

    query_sums = jnp.sum(projected_grad[:head_width].astype(F32), axis=1)
    value_sums = jnp.sum(projected_grad[2 * head_width :].astype(F32), axis=1)
    put = lambda size, part: lax.dynamic_update_slice_in_dim(
        jnp.zeros((size,), F32), part, me * part.shape[0], axis=0
    )
    bias_local = jnp.concatenate(
        [
            put(width, query_sums),
            put(width, value_sums),
            jnp.sum(branch1_grad.astype(F32), axis=0),
            put(hidden_width, jnp.sum(before_grad.astype(F32), axis=0)),
            jnp.sum(branch2_grad_all[:rows].astype(F32), axis=0),
        ]
    )
    bias_sum = halve_all(bias_local.reshape(n_wide, -1), stages, "wide", n_wide, wide, F32)
    bias_sum = bias_sum.reshape(n_narrow, -1)
    bias_sum = halve_all(
        bias_sum, n_narrow.bit_length() - 1, "narrow", n_narrow, me, F32
    )
    return (
        output,
        tokens_grad,
        conditions_grad,
        ada_weight_grad,
        ada_bias_grad,
        qkv_flat.astype(F32).reshape(1, -1),
        bias_sum.reshape(-1),
        proj_flat.reshape(1, -1),
        fc1_flat.reshape(1, -1),
        fc2_flat.reshape(1, -1),
    )


def nn_t(a, b):
    return nt(a, b)


def reduce_tokens(part, rows, n_narrow):
    return scatter_relative(
        part[:rows],
        [part[j * rows : (j + 1) * rows] for j in range(1, n_narrow)],
        "narrow",
        n_narrow,
    )


def solution(mesh):
    placed = (
        P(("wide", "narrow"), None),
        P("wide", None),
        P(("wide", "narrow")),
        P(("wide", "narrow")),
        P("wide", None),
        P(None, "narrow"),
        P("narrow"),
        P(),
        P(),
        P(),
        P(),
        P(),
        P(("wide", "narrow"), None),
    )
    return jax.shard_map(
        functools.partial(body, mesh.shape["wide"], mesh.shape["narrow"]),
        mesh=mesh,
        in_specs=placed,
        out_specs=(
            P(("wide", "narrow"), None),
            P(("wide", "narrow"), None),
            P("wide", "narrow"),
            P(None, "narrow"),
            P("narrow"),
            P("narrow", "wide"),
            P(("wide", "narrow")),
            P("narrow", "wide"),
            P("narrow", "wide"),
            P("narrow", "wide"),
        ),
        check_vma=False,
    )
```

```python
import functools
import math

import jax
import jax.numpy as jnp
from jax import lax
from jax.experimental import pallas as pl
from jax.experimental.pallas import tpu as pltpu
from jax.sharding import PartitionSpec as P

HEADS = 16
HEAD = 72
BIG = 1024
SMALL = 256
EPSILON = 1e-06
MASKED = -1e30
FACTOR = HEAD ** (-0.5)
LOG2E = math.log2(math.e)
BF16 = jnp.bfloat16
F32 = jnp.float32


def swap(x, axis, size, mask):
    return lax.ppermute(x, axis, [(i, i ^ mask) for i in range(size)])


def gather_relative(x, axis, size):
    out = x[None]
    mask = 1
    while mask < size:
        out = jnp.concatenate([out, swap(out, axis, size, mask)], axis=0)
        mask *= 2
    return out


def scatter_relative(mine, others, axis, size):
    total = mine.astype(F32)
    for j in range(1, size):
        total = total + swap(others[j - 1].astype(BF16), axis, size, j).astype(F32)
    return total


def absolute(blocks, me, size):
    if size == 2:
        return jnp.where(me == 0, blocks, blocks[::-1])
    return jnp.take(blocks, jnp.arange(size) ^ me, axis=0)


def halve(y, place, bit, axis, size, index, kind, anchor=None):
    mine = (index >> bit) & 1
    keep = y if anchor is None else after(y, anchor)
    keep = lax.dynamic_index_in_dim(keep, mine, place, keepdims=False)
    send = lax.dynamic_index_in_dim(y, 1 - mine, place, keepdims=False)
    got = swap(send.astype(kind), axis, size, 1 << bit)
    return (keep.astype(F32) + got.astype(F32)).astype(kind)


def split_bits(y, count):
    return y.reshape((2,) * count + (y.shape[0] >> count,) + y.shape[1:])


def halve_first(y, bit, n_wide, wide, anchor):
    return halve(y, y.ndim - 3, bit, "wide", n_wide, wide, BF16, anchor)


def halve_all(y, count, axis, size, index, kind):
    y = y.reshape((2,) * count + (y.shape[0] >> count,) + y.shape[1:])
    for bit in range(count):
        y = halve(y, count - 1 - bit, bit, axis, size, index, kind)
    return y


def rows_to_columns(y, n_wide, n_narrow, hi):
    repeat = n_wide // n_narrow
    width = y.shape[1] // n_narrow
    blocks = jnp.stack([y[:, i * width : (i + 1) * width] for i in range(n_narrow)])
    total = None
    for k in range(n_narrow):
        pairs = []
        for h in range(n_narrow):
            for j in range(repeat):
                for n in range(n_narrow):
                    source = (h * repeat + j) * n_narrow + n
                    target = (n * repeat + j) * n_narrow + (h + k) % n_narrow
                    pairs.append((source, target))
        send = lax.dynamic_index_in_dim(blocks, (hi + k) % n_narrow, 0, keepdims=False)
        got = lax.ppermute(send, ("wide", "narrow"), pairs).astype(F32)
        total = got if total is None else total + got
    return total


TILE = 256


def fill_mask(row_ref, col_ref, mask_ref):
    col = col_ref[0]
    row = row_ref[0]
    shape = (BIG, BIG)
    same = (col >> 1) == (row >> 1)
    own = lax.broadcasted_iota(jnp.int32, shape, 0) == lax.broadcasted_iota(jnp.int32, shape, 1)
    usable = jnp.broadcast_to((col & 1) == 1, shape) | own
    mask_ref[...] = jnp.where(same & usable, 0.0, MASKED)


def nn(a, b):
    return lax.dot_general(a, b, (((1,), (0,)), ((), ())), preferred_element_type=F32)


def nt(a, b):
    return lax.dot_general(a, b, (((1,), (1,)), ((), ())), preferred_element_type=F32)


def tn(a, b):
    return lax.dot_general(a, b, (((0,), (0,)), ((), ())), preferred_element_type=F32)


FORWARD_TILE = 512


def forward_kernel(q_ref, k_ref, v_ref, row_ref, col_ref, o_ref, l_ref, mask_ref):
    @pl.when(pl.program_id(1) == 0)
    def _():
        fill_mask(row_ref, col_ref, mask_ref)

    keys = k_ref[0, 0].T
    values = v_ref[0, 0]
    parts = [slice(i, i + FORWARD_TILE) for i in range(0, BIG, FORWARD_TILE)]

    def scores_of(part):
        return nn(keys, q_ref[0, 0, :, part]) * (FACTOR * LOG2E) + mask_ref[:, part]

    following = scores_of(parts[0])
    for place, part in enumerate(parts):
        scores = following
        if place + 1 < len(parts):
            following = scores_of(parts[place + 1])
        top = jnp.max(scores, axis=0, keepdims=True)
        weights = jnp.exp2(scores - top)
        total = jnp.sum(weights, axis=0, keepdims=True)
        mixed = nn(values, weights.astype(BF16))
        o_ref[0, :, part] = (mixed * (1.0 / total)).astype(BF16)
        l_ref[0, :, part] = top + jnp.log2(total)


def backward_kernel(
    q_ref, k_ref, v_ref, g_ref, o_ref, l_ref, row_ref, col_ref, d_ref, mask_ref
):
    @pl.when(pl.program_id(1) == 0)
    def _():
        fill_mask(row_ref, col_ref, mask_ref)

    keys_t = k_ref[0, 0]
    keys = keys_t.T
    values = v_ref[0, 0].T
    key_grad = jnp.zeros((BIG, HEAD), F32)
    value_grad = jnp.zeros((BIG, HEAD), F32)
    parts = [slice(i, i + TILE) for i in range(0, BIG, TILE)]

    def products_of(part):
        return nn(keys, q_ref[0, 0, :, part]), nn(values, g_ref[0, :, part])

    following = products_of(parts[0])
    for place, part in enumerate(parts):
        product, prob_grad = following
        if place + 1 < len(parts):
            following = products_of(parts[place + 1])
        queries = q_ref[0, 0, :, part]
        grads = g_ref[0, :, part]
        delta = jnp.sum(
            grads.astype(F32) * o_ref[0, :, part].astype(F32), axis=0, keepdims=True
        )
        scores = product * (FACTOR * LOG2E) + mask_ref[:, part]
        probs = jnp.exp2(scores - l_ref[0, :, part])
        score_grad = (probs * (prob_grad - delta)).astype(BF16)
        value_grad = value_grad + nt(probs.astype(BF16), grads)
        key_grad = key_grad + nt(score_grad, queries)
        d_ref[0, 0, :, part] = (nn(keys_t, score_grad) * FACTOR).astype(BF16)
    d_ref[1, 0] = (key_grad * FACTOR).T.astype(BF16)
    d_ref[2, 0] = value_grad.T.astype(BF16)


def projected_spec(kind, first=0):
    return pl.BlockSpec((1, 1, HEAD, BIG), lambda c, h: (kind, first + h, 0, c))


def label_operands(labels):
    chunks = labels.shape[0] // BIG
    return labels.reshape(chunks, 1, BIG), labels.reshape(chunks, BIG, 1)


LABEL_SPECS = [
    pl.BlockSpec((1, 1, BIG), lambda c, h: (c, 0, 0)),
    pl.BlockSpec((1, BIG, 1), lambda c, h: (c, 0, 0)),
]
WIDE_SPEC = pl.BlockSpec((1, HEAD, BIG), lambda c, h: (h, 0, c))
LINE_SPEC = pl.BlockSpec((1, 1, BIG), lambda c, h: (h, 0, c))


def attend_forward(projected, labels, first, heads):
    count = projected.shape[3]
    return pl.pallas_call(
        forward_kernel,
        grid=(count // BIG, heads),
        in_specs=[projected_spec(kind, first) for kind in range(3)] + LABEL_SPECS,
        out_specs=[WIDE_SPEC, LINE_SPEC],
        out_shape=[
            jax.ShapeDtypeStruct((heads, HEAD, count), BF16),
            jax.ShapeDtypeStruct((heads, 1, count), F32),
        ],
        scratch_shapes=[pltpu.VMEM((BIG, BIG), F32)],
        name="attend_forward",
    )(projected, projected, projected, *label_operands(labels))


def attend_backward(projected, grads, attended, log_total, labels, first):
    heads = log_total.shape[0]
    count = projected.shape[3]
    return pl.pallas_call(
        backward_kernel,
        grid=(count // BIG, heads),
        in_specs=[projected_spec(kind, first) for kind in range(3)]
        + [pl.BlockSpec((1, HEAD, BIG), lambda c, h: (first + h, 0, c))]
        + [WIDE_SPEC, LINE_SPEC]
        + LABEL_SPECS,
        out_specs=pl.BlockSpec((3, 1, HEAD, BIG), lambda c, h: (0, h, 0, c)),
        out_shape=jax.ShapeDtypeStruct((3, heads, HEAD, count), BF16),
        scratch_shapes=[pltpu.VMEM((BIG, BIG), F32)],
        name="attend_backward",
    )(projected, projected, projected, grads, attended, log_total, *label_operands(labels))


def normalise(values):
    centred = values - jnp.mean(values, axis=-1, keepdims=True)
    scale = lax.rsqrt(jnp.mean(centred * centred, axis=-1, keepdims=True) + EPSILON)
    return centred * scale, scale


def normalise_back(normed, scale, grad):
    return scale * (
        grad
        - jnp.mean(grad, axis=-1, keepdims=True)
        - normed * jnp.mean(grad * normed, axis=-1, keepdims=True)
    )


def row_spec(width, offset=0):
    return pl.BlockSpec((SMALL, width), lambda i: (offset + i, 0))


def piece_spec(piece, width, offset=0):
    return pl.BlockSpec((1, 1, width), lambda i: (offset + i, 0, piece))


def sums_spec(count, width):
    return pl.BlockSpec((1, count, width), lambda i: (i, 0, 0))


def column_sum(values):
    return jnp.sum(values, axis=0, keepdims=True)


def first_kernel(x_ref, shift_ref, scale_ref, *rest):
    normed, _ = normalise(x_ref[...].astype(F32))
    rest[-1][...] = (normed * (1.0 + scale_ref[0]) + shift_ref[0]).T.astype(BF16)


def first_norm(shards, per_block):
    rows, width = shards[0].shape
    blocks = rows // SMALL
    out = None
    for place, shard in enumerate(shards):
        offset = place * blocks
        out = pl.pallas_call(
            first_kernel,
            grid=(blocks,),
            in_specs=[row_spec(width), piece_spec(0, width, offset), piece_spec(1, width, offset)]
            + ([] if out is None else [pl.BlockSpec(memory_space=pl.ANY)]),
            out_specs=pl.BlockSpec((width, SMALL), lambda i, offset=offset: (0, offset + i)),
            out_shape=jax.ShapeDtypeStruct((width, rows * len(shards)), BF16),
            input_output_aliases={} if out is None else {3: 0},
            name="first_norm",
        )(shard, per_block, per_block, *([] if out is None else [out]))
    return out


def second_kernel(count, me_ref, *refs):
    parts = refs[:count]
    weight_ref, bias_ref, gate_ref, shift_ref, scale_ref, x_ref = refs[count : count + 6]
    branch_ref, middle_ref, o_ref, ordered_ref = refs[count + 6 :]
    for place, part_ref in enumerate(parts):
        ordered_ref[((me_ref[0] ^ (place // 2)) * 2) + place % 2] = part_ref[...]
    ordered = ordered_ref[...].reshape(weight_ref.shape[0], SMALL)
    branch = tn(ordered, weight_ref[...]) + bias_ref[...]
    middle = x_ref[...].astype(F32) + gate_ref[0] * branch
    normed, _ = normalise(middle)
    branch_ref[...] = branch
    middle_ref[...] = middle
    o_ref[...] = (normed * (1.0 + scale_ref[0]) + shift_ref[0]).astype(BF16)


def second_norm(parts, me, proj_weight, bias, per_block, tokens_all, rows):
    count, width = tokens_all.shape
    blocks = count // SMALL
    own = rows // SMALL
    features = parts[0].shape[0]
    n_parts = len(parts)

    def turned(i):
        return blocks - 1 - i

    def part_spec(place):
        def index(i, me_ref):
            block = turned(i)
            return (0, ((block // own) ^ (place // 2)) * own + block % own)

        return pl.BlockSpec((features, SMALL), index)

    def piece(kind):
        return pl.BlockSpec((1, 1, width), lambda i, me_ref: (turned(i), 0, kind))

    kept = pl.BlockSpec((SMALL, width), lambda i, me_ref: (jnp.minimum(turned(i), own - 1), 0))
    all_rows = pl.BlockSpec((SMALL, width), lambda i, me_ref: (turned(i), 0))
    return pl.pallas_call(
        functools.partial(second_kernel, n_parts),
        grid_spec=pltpu.PrefetchScalarGridSpec(
            num_scalar_prefetch=1,
            grid=(blocks,),
            in_specs=[part_spec(p) for p in range(n_parts)]
            + [
                pl.BlockSpec((n_parts * features, width), lambda i, me_ref: (0, 0)),
                pl.BlockSpec((1, width), lambda i, me_ref: (0, 0)),
                piece(2),
                piece(3),
                piece(4),
                all_rows,
            ],
            out_specs=[kept, kept, all_rows],
            scratch_shapes=[pltpu.VMEM((n_parts, features, SMALL), BF16)],
        ),
        out_shape=[
            jax.ShapeDtypeStruct((rows, width), F32),
            jax.ShapeDtypeStruct((rows, width), F32),
            jax.ShapeDtypeStruct((count, width), BF16),
        ],
        name="second_norm",
    )(
        me.reshape(1),
        *parts,
        proj_weight,
        bias,
        per_block,
        per_block,
        per_block,
        tokens_all,
    )


def added(refs):
    total = refs[0][...].astype(F32)
    for ref in refs[1:]:
        total = total + ref[...].astype(F32)
    return total


def second_back_kernel(count, *refs):
    middle_ref, branch_ref, g_ref, gate_ref, scale_ref = refs[count : count + 5]
    d_ref, b_ref, s_ref = refs[count + 5 :]
    grad = added(refs[:count])
    normed, ratio = normalise(middle_ref[...])
    total = g_ref[...].astype(F32) + normalise_back(normed, ratio, grad * (1.0 + scale_ref[0]))
    branch_grad = (gate_ref[0] * total).astype(BF16)
    d_ref[...] = total
    b_ref[...] = branch_grad
    s_ref[0] = jnp.concatenate(
        [
            column_sum(total * branch_ref[...]),
            column_sum(grad),
            column_sum(grad * normed),
            column_sum(branch_grad.astype(F32)),
        ],
        axis=0,
    )


def second_back(parts, middle, branch1, output_grad, per_block):
    rows, width = middle.shape
    blocks = rows // SMALL
    return pl.pallas_call(
        functools.partial(second_back_kernel, len(parts)),
        grid=(blocks,),
        in_specs=[row_spec(width)] * (len(parts) + 3)
        + [piece_spec(2, width), piece_spec(4, width)],
        out_specs=[row_spec(width), row_spec(width), sums_spec(4, width)],
        out_shape=[
            jax.ShapeDtypeStruct((rows, width), F32),
            jax.ShapeDtypeStruct((rows, width), BF16),
            jax.ShapeDtypeStruct((blocks, 4, width), F32),
        ],
        name="second_back",
    )(*parts, middle, branch1, output_grad, per_block, per_block)


def output_kernel(count, *refs):
    middle_ref, g_ref, gate_ref, bias_ref, o_ref, s_ref = refs[count:]
    branch = added(refs[:count]) + bias_ref[...]
    grad = g_ref[...].astype(F32)
    o_ref[...] = (middle_ref[...] + gate_ref[0] * branch).astype(BF16)
    s_ref[0] = jnp.concatenate(
        [
            column_sum(grad * branch),
            column_sum((gate_ref[0] * grad).astype(BF16).astype(F32)),
        ],
        axis=0,
    )


def finish_output(parts, middle, output_grad, per_block, bias):
    rows, width = middle.shape
    blocks = rows // SMALL
    return pl.pallas_call(
        functools.partial(output_kernel, len(parts)),
        grid=(blocks,),
        in_specs=[row_spec(width)] * (len(parts) + 2)
        + [piece_spec(5, width), pl.BlockSpec((1, width), lambda i: (0, 0))],
        out_specs=[row_spec(width), sums_spec(2, width)],
        out_shape=[
            jax.ShapeDtypeStruct((rows, width), BF16),
            jax.ShapeDtypeStruct((blocks, 2, width), F32),
        ],
        name="finish_output",
    )(*parts, middle, output_grad, per_block, bias)


def first_sums_kernel(part_ref, x_ref, s_ref):
    grad = part_ref[...].astype(F32)
    normed, _ = normalise(x_ref[...].astype(F32))
    s_ref[0] = jnp.concatenate([column_sum(grad), column_sum(grad * normed)], axis=0)


def first_sums(part, tokens_all):
    count, width = tokens_all.shape
    return pl.pallas_call(
        first_sums_kernel,
        grid=(count // SMALL,),
        in_specs=[row_spec(width)] * 2,
        out_specs=sums_spec(2, width),
        out_shape=jax.ShapeDtypeStruct((count // SMALL, 2, width), F32),
        name="first_sums",
    )(part, tokens_all)


def first_back_kernel(count, *refs):
    x_ref, d_ref, scale_ref, o_ref = refs[count:]
    grad = added(refs[:count])
    normed, ratio = normalise(x_ref[...].astype(F32))
    o_ref[...] = d_ref[...] + normalise_back(normed, ratio, grad * (1.0 + scale_ref[0]))


def first_back(parts, tokens, middle_grad, per_block):
    rows, width = tokens.shape
    return pl.pallas_call(
        functools.partial(first_back_kernel, len(parts)),
        grid=(rows // SMALL,),
        in_specs=[row_spec(width)] * (len(parts) + 2) + [piece_spec(1, width)],
        out_specs=row_spec(width),
        out_shape=jax.ShapeDtypeStruct((rows, width), F32),
        name="first_back",
    )(*parts, tokens, middle_grad, per_block)


def blocked(x):
    return x.reshape(x.shape[0] // SMALL, SMALL, x.shape[1])


def flat(x):
    return x.reshape(x.shape[0] * x.shape[1], x.shape[2])


def nt_of(a, b):
    return lax.dot_general(a, b, (((0,), (1,)), ((), ())), preferred_element_type=F32)


def after(x, *others):
    return lax.optimization_barrier((x,) + others)[0]


def received(others, n_narrow):
    return [
        swap(other, "narrow", n_narrow, j) for j, other in enumerate(others, start=1)
    ]


def row_shards(x, rows, axis):
    return [
        lax.slice_in_dim(x, j * rows, (j + 1) * rows, axis=axis)
        for j in range(x.shape[axis] // rows)
    ]


def shards_of(x, n_narrow):
    out = [x]
    mask = 1
    while mask < n_narrow:
        out = out + [swap(o, "narrow", n_narrow, mask) for o in out]
        mask *= 2
    return out


def body(
    n_wide,
    n_narrow,
    tokens,
    conditions,
    segment_ids,
    pad_mask,
    segment_image,
    ada_weight,
    ada_bias,
    qkv_weight,
    trunk_bias,
    proj_weight,
    fc1_weight,
    fc2_weight,
    output_grad,
):
    rows, width = tokens.shape
    hidden_width = fc1_weight.shape[1]
    me = lax.axis_index("narrow")
    wide = lax.axis_index("wide")
    stages = n_wide.bit_length() - 1
    low_stages = (n_wide // n_narrow).bit_length() - 1
    hi = wide >> low_stages
    heads = HEADS // n_narrow
    half_heads = heads // 2
    head_width = heads * HEAD
    fc_width = hidden_width // n_narrow
    own_blocks = rows // SMALL
    image_count = conditions.shape[0]
    biases = trunk_bias.astype(F32)
    query_bias = biases[:width]
    value_bias = biases[width : 2 * width]
    proj_bias = biases[2 * width : 3 * width][None, :]
    first_bias = biases[3 * width : 3 * width + hidden_width]
    second_bias = biases[3 * width + hidden_width :][None, :]
    mine_of = functools.partial(lax.dynamic_slice_in_dim, axis=0)

    token_shards = shards_of(tokens, n_narrow)
    labels = gather_relative(segment_ids * 2 + pad_mask, "narrow", n_narrow).reshape(-1)
    grad_shards = shards_of(after(output_grad, token_shards[-1]), n_narrow)

    conditions32 = conditions.astype(F32)
    act = jax.nn.silu(conditions32).astype(BF16)
    columns = (
        jnp.dot(act, ada_weight, preferred_element_type=F32) + ada_bias.astype(F32)
    ).astype(BF16)
    modulation = absolute(gather_relative(columns, "narrow", n_narrow), me, n_narrow)
    modulation = modulation.transpose(1, 0, 2).reshape(image_count, -1)
    slots = labels[::SMALL] >> 1
    image = jnp.sum(
        jnp.where(
            slots[:, None] == jnp.arange(image_count, dtype=jnp.int32)[None, :],
            segment_image[0][None, :],
            0,
        ),
        axis=1,
    )
    pick = image[:, None] == jnp.arange(image_count, dtype=jnp.int32)[None, :]
    per_block = jnp.dot(pick.astype(BF16), modulation, preferred_element_type=F32)[:, None, :]

    qkv_mine = lax.dynamic_slice_in_dim(
        qkv_weight.reshape(width, 3, width), me * head_width, head_width, axis=2
    ).reshape(width, 3 * head_width)
    qkv_bias = jnp.concatenate(
        [
            mine_of(query_bias, me * head_width, head_width),
            jnp.zeros((head_width,), F32),
            mine_of(value_bias, me * head_width, head_width),
        ]
    )
    first_in_all = first_norm(token_shards, per_block)
    tokens_all = jnp.concatenate(token_shards, axis=0)
    projected = (tn(qkv_mine, first_in_all) + qkv_bias[:, None]).astype(BF16)
    projected = projected.reshape(3, heads, HEAD, -1)
    attended0, log_total0 = attend_forward(projected, labels, 0, half_heads)
    attended1, log_total1 = attend_forward(
        after(projected, attended0), labels, half_heads, half_heads
    )
    half_width = half_heads * HEAD
    attended = [attended0.reshape(half_width, -1), attended1.reshape(half_width, -1)]
    gathered = [shards_of(a, n_narrow) for a in attended]

    fc1_mine = lax.dynamic_slice_in_dim(fc1_weight, me * fc_width, fc_width, axis=1)
    fc2_mine = lax.dynamic_slice_in_dim(fc2_weight, me * fc_width, fc_width, axis=0)
    output_grad_all = after(jnp.concatenate(grad_shards, axis=0), attended1)
    gate2 = per_block[:, :, 5 * width :]
    branch2_grad_all = flat(gate2 * blocked(output_grad_all.astype(F32))).astype(BF16)
    hidden_grad = nt(branch2_grad_all, fc2_mine)

    branch1, middle, second_in_all = second_norm(
        [gathered[s][j] for j in range(n_narrow) for s in range(2)],
        me,
        proj_weight,
        proj_bias,
        per_block,
        after(tokens_all, hidden_grad),
        rows,
    )

    before = nn(second_in_all, fc1_mine) + mine_of(first_bias, me * fc_width, fc_width)
    hidden, gelu_pull = jax.vjp(lambda v: jax.nn.gelu(v, approximate=True), before)
    hidden = hidden.astype(BF16)
    before_grad = gelu_pull(hidden_grad)[0].astype(BF16)
    own_grad, *other_grads = row_shards(before_grad, rows, 0)
    second_in_others = [nt(g, fc1_mine).astype(BF16) for g in other_grads]
    second_in_mine = nt(after(own_grad, *second_in_others), fc1_mine)
    second_in_parts = [second_in_mine] + received(second_in_others, n_narrow)
    fc2_local = tn(after(hidden, second_in_mine), branch2_grad_all).astype(BF16)
    fc1_local = tn(after(second_in_all, fc2_local), before_grad).astype(BF16)

    fc2_sum = split_bits(fc2_local, low_stages)
    fc1_sum = split_bits(fc1_local, stages)
    halved = functools.partial(halve_first, n_wide=n_wide, wide=wide)
    fc2_sum = halved(fc2_sum, 0, anchor=fc1_local)

    middle_grad, branch1_grad, second_sums = second_back(
        second_in_parts, after(middle, fc2_sum), branch1, output_grad, per_block
    )
    branch1_grad_all = jnp.concatenate(shards_of(branch1_grad, n_narrow), axis=0)
    own_hidden, *other_hidden = row_shards(after(hidden, branch1_grad), rows, 0)
    branch2_others = [nn(h, fc2_mine).astype(BF16) for h in other_hidden]
    branch2_mine = nn(own_hidden, fc2_mine)
    fc1_sum = halved(fc1_sum, 0, anchor=(branch2_mine, branch2_others))
    branch1_grad_all = after(branch1_grad_all, fc1_sum)
    proj_mine = lax.dynamic_slice_in_dim(proj_weight, me * head_width, head_width, axis=0)
    attended_grad = nt(proj_mine, branch1_grad_all).astype(BF16).reshape(heads, HEAD, -1)
    fc2_sum = halved(fc2_sum, 1, anchor=attended_grad)
    projected_grad0 = attend_backward(
        projected, after(attended_grad, fc2_sum), attended0, log_total0, labels, 0
    )
    branch2_parts = [branch2_mine] + received(
        [after(b, branch1_grad_all) for b in branch2_others], n_narrow
    )
    proj_local = jnp.concatenate(
        [nn(after(a, projected_grad0), branch1_grad_all).astype(BF16) for a in attended], axis=0
    )
    proj_sum = split_bits(proj_local, low_stages)
    grad0 = projected_grad0.reshape(3 * half_width, -1)
    qkv0_sum = split_bits(nt(first_in_all, grad0).astype(BF16), stages)
    for bit in range(2, low_stages):
        fc2_sum = halved(fc2_sum, bit, anchor=projected_grad0)
    fc1_sum = halved(fc1_sum, 1, anchor=projected_grad0)
    projected_grad1 = attend_backward(
        projected,
        after(attended_grad, fc2_sum, fc1_sum, proj_sum, qkv0_sum),
        attended1,
        log_total1,
        labels,
        half_heads,
    )
    grad1 = projected_grad1.reshape(3 * half_width, -1)

    qkv0_sum = halved(qkv0_sum, 0, anchor=projected_grad1)
    projected_grad = jnp.concatenate([projected_grad0, projected_grad1], axis=1)
    projected_grad = after(projected_grad.reshape(3 * head_width, -1), qkv0_sum)
    grad_shards1 = row_shards(projected_grad, rows, 1)
    first_in_others = [nt_of(g, qkv_mine).astype(BF16) for g in grad_shards1[1:]]
    first_in_arrived = received(first_in_others, n_narrow)
    qkv1_sum = split_bits(
        nt(after(first_in_all, *first_in_others), grad1).astype(BF16), stages
    )
    proj_sum = halved(proj_sum, 0, anchor=qkv1_sum)
    first_in_mine = nt_of(after(grad_shards1[0], proj_sum), qkv_mine)
    for bit in range(2, stages - 1):
        fc1_sum = halved(fc1_sum, bit, anchor=first_in_mine)

    first_block_sums = jnp.concatenate(
        [first_sums(g, x) for g, x in zip([first_in_mine] + first_in_others, token_shards)],
        axis=0,
    )
    qkv1_sum = halved(qkv1_sum, 0, anchor=first_block_sums)
    qkv0_sum = halved(qkv0_sum, 1, anchor=first_block_sums)
    output, output_sums = finish_output(
        branch2_parts,
        middle,
        after(output_grad, projected_grad0),
        per_block,
        second_bias,
    )

    def by_image(choice, sums):
        return lax.dot_general(
            choice.astype(F32),
            sums.reshape(sums.shape[0], -1),
            (((0,), (0,)), ((), ())),
            precision=lax.Precision.HIGHEST,
            preferred_element_type=F32,
        )

    modulation_part = jnp.concatenate(
        [
            by_image(pick, first_block_sums),
            by_image(pick[:own_blocks], second_sums[:, :3]),
            by_image(pick[:own_blocks], output_sums[:, :1]),
        ],
        axis=1,
    )
    modulation_part = modulation_part.reshape(image_count, n_narrow, -1).transpose(1, 0, 2)

    def put(size, part):
        return lax.dynamic_update_slice_in_dim(
            jnp.zeros((size,), F32), part, me * part.shape[0], axis=0
        )

    def line_sums(first):
        return jnp.concatenate(
            [
                jnp.sum(g[first : first + half_width].astype(F32), axis=1)
                for g in (grad0, grad1)
            ]
        )

    bias_local = jnp.concatenate(
        [
            put(width, line_sums(0)),
            put(width, line_sums(2 * half_width)),
            jnp.sum(second_sums[:, 3], axis=0),
            put(hidden_width, jnp.sum(before_grad.astype(F32), axis=0)),
            jnp.sum(output_sums[:, 1], axis=0),
        ]
    )
    bias_width = bias_local.shape[0] // (n_wide * n_narrow)
    bias_local = bias_local.reshape(n_wide, n_narrow, bias_width).transpose(1, 0, 2)
    small = jnp.concatenate(
        [modulation_part, bias_local.reshape(n_narrow, image_count, -1)], axis=2
    )
    relative = absolute(small, me, n_narrow)
    small = scatter_relative(
        relative[0], [relative[j] for j in range(1, n_narrow)], "narrow", n_narrow
    ).astype(BF16)
    column_count = small.shape[1] - n_wide * bias_width // image_count
    modulation_grad = small[:, :column_count]
    together = gather_relative(jnp.concatenate([small, act], axis=1), "wide", n_wide)
    bias_sum = jnp.sum(together[:, :, column_count:-width].astype(F32), axis=0)
    bias_sum = lax.dynamic_index_in_dim(
        bias_sum.reshape(n_wide, bias_width), wide, 0, keepdims=False
    )
    together = together.reshape(n_wide * image_count, -1)
    modulation_grad_all = together[:, :column_count]
    ada_weight_grad = tn(together[:, -width:], modulation_grad_all)
    ada_bias_grad = jnp.sum(modulation_grad_all.astype(F32), axis=0)

    for bit in range(1, low_stages):
        proj_sum = halved(proj_sum, bit, anchor=output)
    for bit in range(2, stages):
        qkv0_sum = halved(qkv0_sum, bit, anchor=output)
    tokens_grad = first_back(
        [first_in_mine] + first_in_arrived,
        tokens,
        after(middle_grad, output, qkv1_sum, proj_sum),
        per_block,
    )
    for bit in range(1, stages):
        qkv1_sum = halved(qkv1_sum, bit, anchor=output)
    proj_flat = rows_to_columns(proj_sum, n_wide, n_narrow, hi)
    fc2_flat = rows_to_columns(fc2_sum, n_wide, n_narrow, hi)
    for bit in range(stages - 1, stages):
        fc1_sum = halved(fc1_sum, bit, anchor=output)
    fc1_flat = fc1_sum.astype(F32)
    qkv_sum = jnp.stack([qkv0_sum, qkv1_sum]).reshape(2, -1, 3, half_width)
    qkv_all = absolute(gather_relative(qkv_sum, "narrow", n_narrow), me, n_narrow)
    qkv_all = qkv_all.transpose(2, 3, 0, 1, 4).reshape(qkv_sum.shape[1], 3 * width)
    qkv_block = 3 * width // n_narrow
    qkv_flat = lax.dynamic_slice_in_dim(qkv_all, me * qkv_block, qkv_block, axis=1)

    act_part = nt(modulation_grad, ada_weight)
    act_part = act_part.reshape(image_count, n_narrow, -1).transpose(1, 0, 2)
    relative = absolute(act_part, me, n_narrow)
    act_grad = scatter_relative(
        relative[0], [relative[j] for j in range(1, n_narrow)], "narrow", n_narrow
    )
    column_width = width // n_narrow
    condition_mine = lax.dynamic_slice_in_dim(conditions32, me * column_width, column_width, 1)
    gate = 1.0 / (1.0 + jnp.exp(-condition_mine))
    conditions_grad = act_grad * (gate * (1.0 + condition_mine * (1.0 - gate)))

    return (
        output,
        tokens_grad,
        conditions_grad,
        ada_weight_grad,
        ada_bias_grad,
        qkv_flat.astype(F32).reshape(1, -1),
        bias_sum.reshape(-1),
        proj_flat.reshape(1, -1),
        fc1_flat.reshape(1, -1),
        fc2_flat.reshape(1, -1),
    )


def solution(mesh):
    placed = (
        P(("wide", "narrow"), None),
        P("wide", None),
        P(("wide", "narrow")),
        P(("wide", "narrow")),
        P("wide", None),
        P(None, "narrow"),
        P("narrow"),
        P(),
        P(),
        P(),
        P(),
        P(),
        P(("wide", "narrow"), None),
    )
    return jax.shard_map(
        functools.partial(body, mesh.shape["wide"], mesh.shape["narrow"]),
        mesh=mesh,
        in_specs=placed,
        out_specs=(
            P(("wide", "narrow"), None),
            P(("wide", "narrow"), None),
            P("wide", "narrow"),
            P(None, "narrow"),
            P("narrow"),
            P("narrow", "wide"),
            P(("wide", "narrow")),
            P("narrow", "wide"),
            P("narrow", "wide"),
            P("narrow", "wide"),
        ),
        check_vma=False,
    )
```

```python
import functools
import math

import jax
import jax.numpy as jnp
from jax import lax
from jax.experimental import pallas as pl
from jax.experimental.pallas import tpu as pltpu
from jax.sharding import PartitionSpec as P


HEADS = 16
HEAD = 72
BIG = 1024
SMALL = 256
EPSILON = 1e-06
MASKED = -1e30
FACTOR = HEAD ** (-0.5)
LOG2E = math.log2(math.e)
BF16 = jnp.bfloat16
F32 = jnp.float32


def swap(x, axis, size, mask):
    return lax.ppermute(x, axis, [(i, i ^ mask) for i in range(size)])


def gather_relative(x, axis, size):
    out = x[None]
    mask = 1
    while mask < size:
        out = jnp.concatenate([out, swap(out, axis, size, mask)], axis=0)
        mask *= 2
    return out


def scatter_relative(mine, others, axis, size):
    total = mine.astype(F32)
    for j in range(1, size):
        total = total + swap(others[j - 1].astype(BF16), axis, size, j).astype(F32)
    return total


def absolute(blocks, me, size):
    if size == 2:
        return jnp.where(me == 0, blocks, blocks[::-1])
    return jnp.take(blocks, jnp.arange(size) ^ me, axis=0)


def halve(y, place, bit, axis, size, index, kind, anchor=None):
    mine = (index >> bit) & 1
    keep = y if anchor is None else after(y, anchor)
    keep = lax.dynamic_index_in_dim(keep, mine, place, keepdims=False)
    send = lax.dynamic_index_in_dim(y, 1 - mine, place, keepdims=False)
    got = swap(send.astype(kind), axis, size, 1 << bit)
    return (keep.astype(F32) + got.astype(F32)).astype(kind)


def split_bits(y, count):
    return y.reshape((2,) * count + (y.shape[0] >> count,) + y.shape[1:])


def halve_first(y, bit, n_wide, wide, anchor):
    return halve(y, y.ndim - 3, bit, "wide", n_wide, wide, BF16, anchor)


def rows_to_columns(y, n_wide, n_narrow, hi):
    repeat = n_wide // n_narrow
    width = y.shape[1] // n_narrow
    blocks = jnp.stack([y[:, i * width : (i + 1) * width] for i in range(n_narrow)])
    total = None
    for k in range(n_narrow):
        pairs = []
        for h in range(n_narrow):
            for j in range(repeat):
                for n in range(n_narrow):
                    source = (h * repeat + j) * n_narrow + n
                    target = (n * repeat + j) * n_narrow + (h + k) % n_narrow
                    pairs.append((source, target))
        send = lax.dynamic_index_in_dim(blocks, (hi + k) % n_narrow, 0, keepdims=False)
        got = lax.ppermute(send, ("wide", "narrow"), pairs).astype(F32)
        total = got if total is None else total + got
    return total


TILE = 256


def fill_mask(row_ref, col_ref, mask_ref):
    col = col_ref[0]
    row = row_ref[0]
    shape = (BIG, BIG)
    same = (col >> 1) == (row >> 1)
    own = lax.broadcasted_iota(jnp.int32, shape, 0) == lax.broadcasted_iota(jnp.int32, shape, 1)
    usable = jnp.broadcast_to((col & 1) == 1, shape) | own
    mask_ref[...] = jnp.where(same & usable, 0.0, MASKED)


def nn(a, b):
    return lax.dot_general(a, b, (((1,), (0,)), ((), ())), preferred_element_type=F32)


def nt(a, b):
    return lax.dot_general(a, b, (((1,), (1,)), ((), ())), preferred_element_type=F32)


def tn(a, b):
    return lax.dot_general(a, b, (((0,), (0,)), ((), ())), preferred_element_type=F32)


FORWARD_TILE = 512


def forward_kernel(q_ref, k_ref, v_ref, row_ref, col_ref, o_ref, l_ref, mask_ref):
    @pl.when(pl.program_id(1) == 0)
    def _():
        fill_mask(row_ref, col_ref, mask_ref)

    keys = k_ref[0, 0].T
    values = v_ref[0, 0]
    parts = [slice(i, i + FORWARD_TILE) for i in range(0, BIG, FORWARD_TILE)]

    def scores_of(part):
        return nn(keys, q_ref[0, 0, :, part]) * (FACTOR * LOG2E) + mask_ref[:, part]

    following = scores_of(parts[0])
    for place, part in enumerate(parts):
        scores = following
        if place + 1 < len(parts):
            following = scores_of(parts[place + 1])
        top = jnp.max(scores, axis=0, keepdims=True)
        weights = jnp.exp2(scores - top)
        total = jnp.sum(weights, axis=0, keepdims=True)
        mixed = nn(values, weights.astype(BF16))
        o_ref[0, :, part] = (mixed * (1.0 / total)).astype(BF16)
        l_ref[0, :, part] = top + jnp.log2(total)


def backward_kernel(
    q_ref, k_ref, v_ref, g_ref, o_ref, l_ref, row_ref, col_ref, d_ref, mask_ref
):
    @pl.when(pl.program_id(1) == 0)
    def _():
        fill_mask(row_ref, col_ref, mask_ref)

    keys_t = k_ref[0, 0]
    keys = keys_t.T
    values = v_ref[0, 0].T
    key_grad = jnp.zeros((BIG, HEAD), F32)
    value_grad = jnp.zeros((BIG, HEAD), F32)
    parts = [slice(i, i + TILE) for i in range(0, BIG, TILE)]

    def products_of(part):
        return nn(keys, q_ref[0, 0, :, part]), nn(values, g_ref[0, :, part])

    following = products_of(parts[0])
    for place, part in enumerate(parts):
        product, prob_grad = following
        if place + 1 < len(parts):
            following = products_of(parts[place + 1])
        queries = q_ref[0, 0, :, part]
        grads = g_ref[0, :, part]
        delta = jnp.sum(
            grads.astype(F32) * o_ref[0, :, part].astype(F32), axis=0, keepdims=True
        )
        scores = product * (FACTOR * LOG2E) + mask_ref[:, part]
        probs = jnp.exp2(scores - l_ref[0, :, part])
        score_grad = (probs * (prob_grad - delta)).astype(BF16)
        value_grad = value_grad + nt(probs.astype(BF16), grads)
        key_grad = key_grad + nt(score_grad, queries)
        d_ref[0, 0, :, part] = (nn(keys_t, score_grad) * FACTOR).astype(BF16)
    d_ref[1, 0] = (key_grad * FACTOR).T.astype(BF16)
    d_ref[2, 0] = value_grad.T.astype(BF16)


def projected_spec(kind, first=0):
    return pl.BlockSpec((1, 1, HEAD, BIG), lambda c, h: (kind, first + h, 0, c))


def label_operands(labels):
    chunks = labels.shape[0] // BIG
    return labels.reshape(chunks, 1, BIG), labels.reshape(chunks, BIG, 1)


LABEL_SPECS = [
    pl.BlockSpec((1, 1, BIG), lambda c, h: (c, 0, 0)),
    pl.BlockSpec((1, BIG, 1), lambda c, h: (c, 0, 0)),
]
WIDE_SPEC = pl.BlockSpec((1, HEAD, BIG), lambda c, h: (h, 0, c))
LINE_SPEC = pl.BlockSpec((1, 1, BIG), lambda c, h: (h, 0, c))


def attend_forward(projected, labels, first, heads):
    count = projected.shape[3]
    return pl.pallas_call(
        forward_kernel,
        grid=(count // BIG, heads),
        in_specs=[projected_spec(kind, first) for kind in range(3)] + LABEL_SPECS,
        out_specs=[WIDE_SPEC, LINE_SPEC],
        out_shape=[
            jax.ShapeDtypeStruct((heads, HEAD, count), BF16),
            jax.ShapeDtypeStruct((heads, 1, count), F32),
        ],
        scratch_shapes=[pltpu.VMEM((BIG, BIG), F32)],
        name="attend_forward",
    )(projected, projected, projected, *label_operands(labels))


def attend_backward(projected, grads, attended, log_total, labels, first):
    heads = log_total.shape[0]
    count = projected.shape[3]
    return pl.pallas_call(
        backward_kernel,
        grid=(count // BIG, heads),
        in_specs=[projected_spec(kind, first) for kind in range(3)]
        + [pl.BlockSpec((1, HEAD, BIG), lambda c, h: (first + h, 0, c))]
        + [WIDE_SPEC, LINE_SPEC]
        + LABEL_SPECS,
        out_specs=pl.BlockSpec((3, 1, HEAD, BIG), lambda c, h: (0, h, 0, c)),
        out_shape=jax.ShapeDtypeStruct((3, heads, HEAD, count), BF16),
        scratch_shapes=[pltpu.VMEM((BIG, BIG), F32)],
        name="attend_backward",
    )(projected, projected, projected, grads, attended, log_total, *label_operands(labels))


def normalise(values):
    centred = values - jnp.mean(values, axis=-1, keepdims=True)
    scale = lax.rsqrt(jnp.mean(centred * centred, axis=-1, keepdims=True) + EPSILON)
    return centred * scale, scale


def normalise_back(normed, scale, grad):
    return scale * (
        grad
        - jnp.mean(grad, axis=-1, keepdims=True)
        - normed * jnp.mean(grad * normed, axis=-1, keepdims=True)
    )


def row_spec(width, offset=0):
    return pl.BlockSpec((SMALL, width), lambda i: (offset + i, 0))


def piece_spec(piece, width, offset=0):
    return pl.BlockSpec((1, 1, width), lambda i: (offset + i, 0, piece))


def sums_spec(count, width):
    return pl.BlockSpec((1, count, width), lambda i: (i, 0, 0))


def column_sum(values):
    return jnp.sum(values, axis=0, keepdims=True)


def first_kernel(x_ref, shift_ref, scale_ref, *rest):
    normed, _ = normalise(x_ref[...].astype(F32))
    modulated = normed * (1.0 + scale_ref[0]) + shift_ref[0]
    rest[-2][...] = modulated.astype(BF16)
    rest[-1][...] = modulated.T.astype(BF16)


def first_norm(shards, per_block):
    rows, width = shards[0].shape
    blocks = rows // SMALL
    out = None
    for place, shard in enumerate(shards):
        offset = place * blocks
        out = pl.pallas_call(
            first_kernel,
            grid=(blocks,),
            in_specs=[row_spec(width), piece_spec(0, width, offset), piece_spec(1, width, offset)]
            + ([] if out is None else [pl.BlockSpec(memory_space=pl.ANY)] * 2),
            out_specs=[
                row_spec(width, offset),
                pl.BlockSpec((width, SMALL), lambda i, offset=offset: (0, offset + i)),
            ],
            out_shape=[
                jax.ShapeDtypeStruct((rows * len(shards), width), BF16),
                jax.ShapeDtypeStruct((width, rows * len(shards)), BF16),
            ],
            input_output_aliases={} if out is None else {3: 0, 4: 1},
            name="first_norm",
        )(shard, per_block, per_block, *([] if out is None else out))
    return out


def second_kernel(count, me_ref, *refs):
    parts = refs[:count]
    weight_ref, bias_ref, gate_ref, shift_ref, scale_ref, x_ref = refs[count : count + 6]
    branch_ref, middle_ref, o_ref, ordered_ref = refs[count + 6 :]
    for place, part_ref in enumerate(parts):
        ordered_ref[((me_ref[0] ^ (place // 2)) * 2) + place % 2] = part_ref[...]
    ordered = ordered_ref[...].reshape(weight_ref.shape[0], SMALL)
    branch = tn(ordered, weight_ref[...]) + bias_ref[...]
    middle = x_ref[...].astype(F32) + gate_ref[0] * branch
    normed, _ = normalise(middle)
    branch_ref[...] = branch
    middle_ref[...] = middle
    o_ref[...] = (normed * (1.0 + scale_ref[0]) + shift_ref[0]).astype(BF16)


def second_norm(parts, me, proj_weight, bias, per_block, tokens_all, rows):
    count, width = tokens_all.shape
    blocks = count // SMALL
    own = rows // SMALL
    features = parts[0].shape[0]
    n_parts = len(parts)

    def turned(i):
        return blocks - 1 - i

    def part_spec(place):
        def index(i, me_ref):
            block = turned(i)
            return (0, ((block // own) ^ (place // 2)) * own + block % own)

        return pl.BlockSpec((features, SMALL), index)

    def piece(kind):
        return pl.BlockSpec((1, 1, width), lambda i, me_ref: (turned(i), 0, kind))

    kept = pl.BlockSpec((SMALL, width), lambda i, me_ref: (jnp.minimum(turned(i), own - 1), 0))
    all_rows = pl.BlockSpec((SMALL, width), lambda i, me_ref: (turned(i), 0))
    return pl.pallas_call(
        functools.partial(second_kernel, n_parts),
        grid_spec=pltpu.PrefetchScalarGridSpec(
            num_scalar_prefetch=1,
            grid=(blocks,),
            in_specs=[part_spec(p) for p in range(n_parts)]
            + [
                pl.BlockSpec((n_parts * features, width), lambda i, me_ref: (0, 0)),
                pl.BlockSpec((1, width), lambda i, me_ref: (0, 0)),
                piece(2),
                piece(3),
                piece(4),
                all_rows,
            ],
            out_specs=[kept, kept, all_rows],
            scratch_shapes=[pltpu.VMEM((n_parts, features, SMALL), BF16)],
        ),
        out_shape=[
            jax.ShapeDtypeStruct((rows, width), F32),
            jax.ShapeDtypeStruct((rows, width), F32),
            jax.ShapeDtypeStruct((count, width), BF16),
        ],
        name="second_norm",
    )(
        me.reshape(1),
        *parts,
        proj_weight,
        bias,
        per_block,
        per_block,
        per_block,
        tokens_all,
    )


def added(refs):
    total = refs[0][...].astype(F32)
    for ref in refs[1:]:
        total = total + ref[...].astype(F32)
    return total


def second_back_kernel(count, *refs):
    middle_ref, branch_ref, g_ref, gate_ref, scale_ref = refs[count : count + 5]
    d_ref, b_ref, s_ref = refs[count + 5 :]
    grad = added(refs[:count])
    normed, ratio = normalise(middle_ref[...])
    total = g_ref[...].astype(F32) + normalise_back(normed, ratio, grad * (1.0 + scale_ref[0]))
    branch_grad = (gate_ref[0] * total).astype(BF16)
    d_ref[...] = total
    b_ref[...] = branch_grad
    s_ref[0] = jnp.concatenate(
        [
            column_sum(total * branch_ref[...]),
            column_sum(grad),
            column_sum(grad * normed),
            column_sum(branch_grad.astype(F32)),
        ],
        axis=0,
    )


def second_back(parts, middle, branch1, output_grad, per_block):
    rows, width = middle.shape
    blocks = rows // SMALL
    return pl.pallas_call(
        functools.partial(second_back_kernel, len(parts)),
        grid=(blocks,),
        in_specs=[row_spec(width)] * (len(parts) + 3)
        + [piece_spec(2, width), piece_spec(4, width)],
        out_specs=[row_spec(width), row_spec(width), sums_spec(4, width)],
        out_shape=[
            jax.ShapeDtypeStruct((rows, width), F32),
            jax.ShapeDtypeStruct((rows, width), BF16),
            jax.ShapeDtypeStruct((blocks, 4, width), F32),
        ],
        name="second_back",
    )(*parts, middle, branch1, output_grad, per_block, per_block)


def output_kernel(count, *refs):
    middle_ref, g_ref, gate_ref, bias_ref, o_ref, s_ref = refs[count:]
    branch = added(refs[:count]) + bias_ref[...]
    grad = g_ref[...].astype(F32)
    o_ref[...] = (middle_ref[...] + gate_ref[0] * branch).astype(BF16)
    s_ref[0] = jnp.concatenate(
        [
            column_sum(grad * branch),
            column_sum((gate_ref[0] * grad).astype(BF16).astype(F32)),
        ],
        axis=0,
    )


def finish_output(parts, middle, output_grad, per_block, bias):
    rows, width = middle.shape
    blocks = rows // SMALL
    return pl.pallas_call(
        functools.partial(output_kernel, len(parts)),
        grid=(blocks,),
        in_specs=[row_spec(width)] * (len(parts) + 2)
        + [piece_spec(5, width), pl.BlockSpec((1, width), lambda i: (0, 0))],
        out_specs=[row_spec(width), sums_spec(2, width)],
        out_shape=[
            jax.ShapeDtypeStruct((rows, width), BF16),
            jax.ShapeDtypeStruct((blocks, 2, width), F32),
        ],
        name="finish_output",
    )(*parts, middle, output_grad, per_block, bias)


def first_sums_kernel(part_ref, x_ref, s_ref):
    grad = part_ref[...].astype(F32)
    normed, _ = normalise(x_ref[...].astype(F32))
    s_ref[0] = jnp.concatenate([column_sum(grad), column_sum(grad * normed)], axis=0)


def first_sums(part, tokens_all):
    count, width = tokens_all.shape
    return pl.pallas_call(
        first_sums_kernel,
        grid=(count // SMALL,),
        in_specs=[row_spec(width)] * 2,
        out_specs=sums_spec(2, width),
        out_shape=jax.ShapeDtypeStruct((count // SMALL, 2, width), F32),
        name="first_sums",
    )(part, tokens_all)


def first_back_kernel(count, *refs):
    x_ref, d_ref, scale_ref, o_ref = refs[count:]
    grad = added(refs[:count])
    normed, ratio = normalise(x_ref[...].astype(F32))
    o_ref[...] = d_ref[...] + normalise_back(normed, ratio, grad * (1.0 + scale_ref[0]))


def first_back(parts, tokens, middle_grad, per_block):
    rows, width = tokens.shape
    return pl.pallas_call(
        functools.partial(first_back_kernel, len(parts)),
        grid=(rows // SMALL,),
        in_specs=[row_spec(width)] * (len(parts) + 2) + [piece_spec(1, width)],
        out_specs=row_spec(width),
        out_shape=jax.ShapeDtypeStruct((rows, width), F32),
        name="first_back",
    )(*parts, tokens, middle_grad, per_block)


def blocked(x):
    return x.reshape(x.shape[0] // SMALL, SMALL, x.shape[1])


def flat(x):
    return x.reshape(x.shape[0] * x.shape[1], x.shape[2])


def nt_of(a, b):
    return lax.dot_general(a, b, (((0,), (1,)), ((), ())), preferred_element_type=F32)


SHARDS = 4


def weight_kernel(core_ref, x_ref, g_ref, keep_ref, send_ref):
    product = nt(x_ref[...], g_ref[...])
    rows = product.shape[0] // SHARDS

    def store(first, second):
        for place in range(SHARDS):
            target = (first, second)[place % 2]
            target[place // 2] = product[place * rows : (place + 1) * rows].astype(BF16)

    @pl.when(core_ref[0] == 0)
    def _():
        store(keep_ref, send_ref)

    @pl.when(core_ref[0] != 0)
    def _():
        store(send_ref, keep_ref)


def weight_halves(turned, grads, wide, n_wide):
    width, count = turned.shape
    rows = width // n_wide
    columns = grads.shape[0]
    block = pl.BlockSpec((SHARDS // 2, rows, columns), lambda i, core: (i, 0, 0))
    shape = jax.ShapeDtypeStruct((n_wide // 2, rows, columns), BF16)
    return pl.pallas_call(
        weight_kernel,
        grid_spec=pltpu.PrefetchScalarGridSpec(
            num_scalar_prefetch=1,
            grid=(n_wide // SHARDS,),
            in_specs=[
                pl.BlockSpec((SHARDS * rows, count), lambda i, core: (i, 0)),
                pl.BlockSpec((columns, count), lambda i, core: (0, 0)),
            ],
            out_specs=[block, block],
        ),
        out_shape=[shape, shape],
        name="weight_halves",
    )((wide & 1).reshape(1), turned, grads)


class Halving:
    def __init__(self, value, bits, n_wide, wide, pair=None):
        self.bits, self.n_wide, self.wide, self.done = bits, n_wide, wide, 0
        self.value = None if value is None else split_bits(value, bits)
        self.pair = pair

    def step(self, anchor, steps=1):
        for _ in range(steps):
            if self.done == self.bits:
                break
            if self.pair is not None:
                keep, send = self.pair
                got = swap(send, "wide", self.n_wide, 1)
                total = after(keep, anchor).astype(F32) + got.astype(F32)
                total = total.astype(BF16)
                self.value = total.reshape((2,) * (self.bits - 1) + total.shape[1:])
                self.pair = None
            else:
                self.value = halve_first(
                    self.value, self.done, self.n_wide, self.wide, anchor
                )
            self.done += 1
        return self.value

    def finish(self, anchor):
        return self.step(anchor, self.bits)


def after(x, *others):
    return lax.optimization_barrier((x,) + others)[0]


def received(others, n_narrow):
    return [
        swap(other, "narrow", n_narrow, j) for j, other in enumerate(others, start=1)
    ]


def row_shards(x, rows, axis):
    return [
        lax.slice_in_dim(x, j * rows, (j + 1) * rows, axis=axis)
        for j in range(x.shape[axis] // rows)
    ]


def shards_of(x, n_narrow):
    out = [x]
    mask = 1
    while mask < n_narrow:
        out = out + [swap(o, "narrow", n_narrow, mask) for o in out]
        mask *= 2
    return out


def body(
    n_wide,
    n_narrow,
    tokens,
    conditions,
    segment_ids,
    pad_mask,
    segment_image,
    ada_weight,
    ada_bias,
    qkv_weight,
    trunk_bias,
    proj_weight,
    fc1_weight,
    fc2_weight,
    output_grad,
):
    rows, width = tokens.shape
    hidden_width = fc1_weight.shape[1]
    me = lax.axis_index("narrow")
    wide = lax.axis_index("wide")
    stages = n_wide.bit_length() - 1
    low_stages = (n_wide // n_narrow).bit_length() - 1
    hi = wide >> low_stages
    heads = HEADS // n_narrow
    half_heads = heads // 2
    head_width = heads * HEAD
    fc_width = hidden_width // n_narrow
    own_blocks = rows // SMALL
    image_count = conditions.shape[0]
    biases = trunk_bias.astype(F32)
    query_bias = biases[:width]
    value_bias = biases[width : 2 * width]
    proj_bias = biases[2 * width : 3 * width][None, :]
    first_bias = biases[3 * width : 3 * width + hidden_width]
    second_bias = biases[3 * width + hidden_width :][None, :]
    mine_of = functools.partial(lax.dynamic_slice_in_dim, axis=0)

    token_shards = shards_of(tokens, n_narrow)
    labels = gather_relative(segment_ids * 2 + pad_mask, "narrow", n_narrow).reshape(-1)
    grad_shards = shards_of(after(output_grad, token_shards[-1]), n_narrow)

    conditions32 = conditions.astype(F32)
    act = jax.nn.silu(conditions32).astype(BF16)
    columns = (
        jnp.dot(act, ada_weight, preferred_element_type=F32) + ada_bias.astype(F32)
    ).astype(BF16)
    modulation = absolute(gather_relative(columns, "narrow", n_narrow), me, n_narrow)
    modulation = modulation.transpose(1, 0, 2).reshape(image_count, -1)
    slots = labels[::SMALL] >> 1
    image = jnp.sum(
        jnp.where(
            slots[:, None] == jnp.arange(image_count, dtype=jnp.int32)[None, :],
            segment_image[0][None, :],
            0,
        ),
        axis=1,
    )
    pick = image[:, None] == jnp.arange(image_count, dtype=jnp.int32)[None, :]
    per_block = jnp.dot(pick.astype(BF16), modulation, preferred_element_type=F32)[:, None, :]

    qkv_mine = lax.dynamic_slice_in_dim(
        qkv_weight.reshape(width, 3, width), me * head_width, head_width, axis=2
    ).reshape(width, 3 * head_width)
    qkv_bias = jnp.concatenate(
        [
            mine_of(query_bias, me * head_width, head_width),
            jnp.zeros((head_width,), F32),
            mine_of(value_bias, me * head_width, head_width),
        ]
    )
    first_in_all, first_in_turned = first_norm(token_shards, per_block)
    tokens_all = jnp.concatenate(token_shards, axis=0)
    projected = (
        lax.dot_general(
            qkv_mine, first_in_all, (((0,), (1,)), ((), ())), preferred_element_type=F32
        )
        + qkv_bias[:, None]
    ).astype(BF16)
    projected = projected.reshape(3, heads, HEAD, -1)
    attended0, log_total0 = attend_forward(projected, labels, 0, half_heads)
    attended1, log_total1 = attend_forward(
        after(projected, attended0), labels, half_heads, half_heads
    )
    half_width = half_heads * HEAD
    attended = [attended0.reshape(half_width, -1), attended1.reshape(half_width, -1)]
    gathered = []
    for part in attended:
        gathered.append(shards_of(part, n_narrow))

    fc1_mine = lax.dynamic_slice_in_dim(fc1_weight, me * fc_width, fc_width, axis=1)
    fc2_mine = lax.dynamic_slice_in_dim(fc2_weight, me * fc_width, fc_width, axis=0)
    output_grad_all = after(jnp.concatenate(grad_shards, axis=0), attended1)
    gate2 = per_block[:, :, 5 * width :]
    branch2_grad_all = flat(gate2 * blocked(output_grad_all.astype(F32))).astype(BF16)
    hidden_grad = nt(branch2_grad_all, fc2_mine)

    branch1, middle, second_in_all = second_norm(
        [gathered[s][j] for j in range(n_narrow) for s in range(2)],
        me,
        proj_weight,
        proj_bias,
        per_block,
        after(tokens_all, hidden_grad),
        rows,
    )

    before = nn(second_in_all, fc1_mine) + mine_of(first_bias, me * fc_width, fc_width)
    hidden, gelu_pull = jax.vjp(lambda v: jax.nn.gelu(v, approximate=True), before)
    hidden = hidden.astype(BF16)
    before_grad = gelu_pull(hidden_grad)[0].astype(BF16)
    own_grad, *other_grads = row_shards(before_grad, rows, 0)
    second_in_others = [nt(g, fc1_mine).astype(BF16) for g in other_grads]
    second_in_mine = nt(after(own_grad, *second_in_others), fc1_mine)
    second_in_parts = [second_in_mine] + received(second_in_others, n_narrow)
    fc2_local = tn(after(hidden, second_in_mine), branch2_grad_all).astype(BF16)
    fc1_local = tn(after(second_in_all, fc2_local), before_grad).astype(BF16)

    fc2_sum = Halving(fc2_local, low_stages, n_wide, wide)
    fc1_sum = Halving(fc1_local, stages, n_wide, wide)
    tied = fc2_sum.step(fc1_local)

    middle_grad, branch1_grad, second_sums = second_back(
        second_in_parts, after(middle, tied), branch1, output_grad, per_block
    )
    branch1_grad_all = jnp.concatenate(shards_of(branch1_grad, n_narrow), axis=0)
    own_hidden, *other_hidden = row_shards(after(hidden, branch1_grad), rows, 0)
    branch2_others = [nn(h, fc2_mine).astype(BF16) for h in other_hidden]
    branch2_mine = nn(own_hidden, fc2_mine)
    tied = fc1_sum.step((branch2_mine, branch2_others))
    branch1_grad_all = after(branch1_grad_all, tied)
    proj_mine = lax.dynamic_slice_in_dim(proj_weight, me * head_width, head_width, axis=0)
    attended_grad = nt(proj_mine, branch1_grad_all).astype(BF16).reshape(heads, HEAD, -1)
    projected_grad0 = attend_backward(
        projected, attended_grad, attended0, log_total0, labels, 0
    )
    branch2_parts = [branch2_mine] + received(
        [after(b, branch1_grad_all) for b in branch2_others], n_narrow
    )
    tied = fc2_sum.step(projected_grad0)
    grad0 = projected_grad0.reshape(3 * half_width, -1)
    qkv0_pair = weight_halves(first_in_turned, after(grad0, tied), wide, n_wide)
    qkv0_sum = Halving(None, stages, n_wide, wide, qkv0_pair)
    proj_local = jnp.concatenate(
        [nn(after(a, qkv0_pair[0]), branch1_grad_all).astype(BF16) for a in attended], axis=0
    )
    proj_sum = Halving(proj_local, low_stages, n_wide, wide)
    output, output_sums = finish_output(
        branch2_parts,
        middle,
        after(output_grad, proj_local),
        per_block,
        second_bias,
    )
    tied = fc1_sum.step(output)

    def put(size, part):
        return lax.dynamic_update_slice_in_dim(
            jnp.zeros((size,), F32), part, me * part.shape[0], axis=0
        )

    def put_half(part):
        return put(width, jnp.concatenate([part, jnp.zeros((half_width,), F32)]))

    bias_local = jnp.concatenate(
        [
            put_half(jnp.sum(grad0[:half_width].astype(F32), axis=1)),
            put_half(jnp.sum(grad0[2 * half_width :].astype(F32), axis=1)),
            jnp.sum(second_sums[:, 3], axis=0),
            put(hidden_width, jnp.sum(before_grad.astype(F32), axis=0)),
            jnp.sum(output_sums[:, 1], axis=0),
        ]
    )
    bias_width = bias_local.shape[0] // (n_wide * n_narrow)
    bias_local = bias_local.reshape(n_wide, n_narrow, bias_width).transpose(1, 0, 2)
    bias_local = bias_local.reshape(n_narrow, image_count, -1)
    projected_grad1 = attend_backward(
        projected,
        after(attended_grad, tied, proj_sum.step(output), bias_local),
        attended1,
        log_total1,
        labels,
        half_heads,
    )
    grad1 = projected_grad1.reshape(3 * half_width, -1)

    tied = qkv0_sum.step(projected_grad1)
    tied = fc2_sum.step(tied)
    projected_grad = jnp.concatenate([projected_grad0, projected_grad1], axis=1)
    projected_grad = after(projected_grad.reshape(3 * head_width, -1), tied)
    grad_shards1 = row_shards(projected_grad, rows, 1)
    first_in_others = [nt_of(g, qkv_mine).astype(BF16) for g in grad_shards1[1:]]
    first_in_arrived = received(first_in_others, n_narrow)
    qkv1_pair = weight_halves(
        first_in_turned, after(grad1, *first_in_others), wide, n_wide
    )
    qkv1_sum = Halving(None, stages, n_wide, wide, qkv1_pair)
    own_grads = after(grad_shards1[0], qkv1_pair[0])
    first_in_mine = nt_of(own_grads, qkv_mine)
    tied = qkv1_sum.step(first_in_mine)

    first_block_sums = [
        first_sums(after(g, tied), x)
        for g, x in zip([first_in_mine] + first_in_others, token_shards)
    ]
    first_block_sums = jnp.concatenate(first_block_sums, axis=0)
    tied = qkv0_sum.step(first_block_sums)

    def by_image(choice, sums):
        return lax.dot_general(
            choice.astype(F32),
            sums.reshape(sums.shape[0], -1),
            (((0,), (0,)), ((), ())),
            precision=lax.Precision.HIGHEST,
            preferred_element_type=F32,
        )

    modulation_part = jnp.concatenate(
        [
            by_image(pick, first_block_sums),
            by_image(pick[:own_blocks], second_sums[:, :3]),
            by_image(pick[:own_blocks], output_sums[:, :1]),
        ],
        axis=1,
    )
    modulation_part = modulation_part.reshape(image_count, n_narrow, -1).transpose(1, 0, 2)

    per_row = n_wide // image_count
    shape = (n_narrow, image_count, per_row * bias_width)
    owner = lax.broadcasted_iota(jnp.int32, shape, 0)
    row = lax.broadcasted_iota(jnp.int32, shape, 1)
    column = lax.broadcasted_iota(jnp.int32, shape, 2) // bias_width
    place = (row * per_row + column) * n_narrow + owner
    for first, base in ((0, 0), (2 * half_width, width)):
        sums = jnp.sum(grad1[first : first + half_width].astype(F32), axis=1)
        start = (base + me * head_width + half_width) // bias_width
        for k in range(half_width // bias_width):
            line = jnp.tile(sums[k * bias_width : (k + 1) * bias_width], per_row)
            bias_local = bias_local + jnp.where(place == start + k, line[None, None, :], 0.0)
    small = jnp.concatenate([modulation_part, bias_local], axis=2)
    relative = absolute(small, me, n_narrow)
    tied = fc1_sum.step(relative)
    small = scatter_relative(
        relative[0], [relative[j] for j in range(1, n_narrow)], "narrow", n_narrow
    ).astype(BF16)
    tokens_grad = first_back(
        [first_in_mine] + first_in_arrived,
        tokens,
        after(middle_grad, relative, qkv0_sum.value, fc1_sum.value),
        per_block,
    )
    column_count = small.shape[1] - n_wide * bias_width // image_count
    modulation_grad = small[:, :column_count]
    together = jnp.concatenate([small, act], axis=1)[None]
    tied = qkv1_sum.step(tokens_grad)
    plan = [
        lambda anchor: (qkv0_sum.step(anchor), proj_sum.step(anchor)),
        lambda anchor: (qkv1_sum.step(anchor),),
        lambda anchor: (qkv0_sum.step(anchor), proj_sum.step(anchor), fc1_sum.step(anchor)),
        lambda anchor: (qkv1_sum.step(anchor),),
    ]
    for stage in range(stages):
        arrived = swap(together, "wide", n_wide, n_wide >> (stage + 1))
        together = jnp.concatenate([after(together, tied), arrived], axis=0)
        if stage == 1:
            modulation_grad = after(modulation_grad, together)
        if stage < len(plan):
            tied = plan[stage](together)
    qkv0_sum.finish(together)
    qkv1_sum.finish(together)
    fc1_sum.finish(together)
    proj_sum.finish(together)
    bias_sum = jnp.sum(together[:, :, column_count:-width].astype(F32), axis=0)
    bias_sum = lax.dynamic_index_in_dim(
        bias_sum.reshape(n_wide, bias_width), wide, 0, keepdims=False
    )
    together = after(together, qkv1_sum.value).reshape(n_wide * image_count, -1)
    modulation_grad_all = together[:, :column_count]
    ada_weight_grad = tn(together[:, -width:], modulation_grad_all)
    ada_bias_grad = jnp.sum(modulation_grad_all.astype(F32), axis=0)

    proj_flat = rows_to_columns(proj_sum.value, n_wide, n_narrow, hi)
    fc2_flat = rows_to_columns(fc2_sum.finish(output), n_wide, n_narrow, hi)
    fc1_flat = fc1_sum.value.astype(F32)
    qkv_sum = jnp.stack([qkv0_sum.value, qkv1_sum.value]).reshape(2, -1, 3, half_width)
    qkv_all = absolute(gather_relative(qkv_sum, "narrow", n_narrow), me, n_narrow)
    qkv_all = qkv_all.transpose(2, 3, 0, 1, 4).reshape(qkv_sum.shape[1], 3 * width)
    qkv_block = 3 * width // n_narrow
    qkv_flat = lax.dynamic_slice_in_dim(qkv_all, me * qkv_block, qkv_block, axis=1)

    act_part = nt(modulation_grad, ada_weight)
    act_part = act_part.reshape(image_count, n_narrow, -1).transpose(1, 0, 2)
    relative = absolute(act_part, me, n_narrow)
    act_grad = scatter_relative(
        relative[0], [relative[j] for j in range(1, n_narrow)], "narrow", n_narrow
    )
    column_width = width // n_narrow
    condition_mine = lax.dynamic_slice_in_dim(conditions32, me * column_width, column_width, 1)
    gate = 1.0 / (1.0 + jnp.exp(-condition_mine))
    conditions_grad = act_grad * (gate * (1.0 + condition_mine * (1.0 - gate)))

    return (
        output,
        tokens_grad,
        conditions_grad,
        ada_weight_grad,
        ada_bias_grad,
        qkv_flat.astype(F32).reshape(1, -1),
        bias_sum.reshape(-1),
        proj_flat.reshape(1, -1),
        fc1_flat.reshape(1, -1),
        fc2_flat.reshape(1, -1),
    )


def solution(mesh):
    placed = (
        P(("wide", "narrow"), None),
        P("wide", None),
        P(("wide", "narrow")),
        P(("wide", "narrow")),
        P("wide", None),
        P(None, "narrow"),
        P("narrow"),
        P(),
        P(),
        P(),
        P(),
        P(),
        P(("wide", "narrow"), None),
    )
    return jax.shard_map(
        functools.partial(body, mesh.shape["wide"], mesh.shape["narrow"]),
        mesh=mesh,
        in_specs=placed,
        out_specs=(
            P(("wide", "narrow"), None),
            P(("wide", "narrow"), None),
            P("wide", "narrow"),
            P(None, "narrow"),
            P("narrow"),
            P("narrow", "wide"),
            P(("wide", "narrow")),
            P("narrow", "wide"),
            P("narrow", "wide"),
            P("narrow", "wide"),
        ),
        check_vma=False,
    )
```

```python
import functools
import math

import jax
import jax.numpy as jnp
from jax import lax
from jax.experimental import pallas as pl
from jax.experimental.pallas import tpu as pltpu
from jax.sharding import PartitionSpec as P


HEADS = 16
HEAD = 72
BIG = 1024
SMALL = 256
EPSILON = 1e-06
MASKED = -1e30
FACTOR = HEAD ** (-0.5)
LOG2E = math.log2(math.e)
BF16 = jnp.bfloat16
F32 = jnp.float32


def swap(x, axis, size, mask):
    return lax.ppermute(x, axis, [(i, i ^ mask) for i in range(size)])


def gather_relative(x, axis, size):
    out = x[None]
    mask = 1
    while mask < size:
        out = jnp.concatenate([out, swap(out, axis, size, mask)], axis=0)
        mask *= 2
    return out


def scatter_relative(mine, others, axis, size):
    total = mine.astype(F32)
    for j in range(1, size):
        total = total + swap(others[j - 1].astype(BF16), axis, size, j).astype(F32)
    return total


def absolute(blocks, me, size):
    if size == 2:
        return jnp.where(me == 0, blocks, blocks[::-1])
    return jnp.take(blocks, jnp.arange(size) ^ me, axis=0)


def halve(y, place, bit, axis, size, index, kind, anchor=None):
    mine = (index >> bit) & 1
    keep = y if anchor is None else after(y, anchor)
    keep = lax.dynamic_index_in_dim(keep, mine, place, keepdims=False)
    send = lax.dynamic_index_in_dim(y, 1 - mine, place, keepdims=False)
    got = swap(send.astype(kind), axis, size, 1 << bit)
    return (keep.astype(F32) + got.astype(F32)).astype(kind)


def split_bits(y, count):
    return y.reshape((2,) * count + (y.shape[0] >> count,) + y.shape[1:])


def halve_first(y, bit, n_wide, wide, anchor):
    return halve(y, y.ndim - 3, bit, "wide", n_wide, wide, BF16, anchor)


def rows_to_columns(y, n_wide, n_narrow, hi):
    repeat = n_wide // n_narrow
    width = y.shape[1] // n_narrow
    blocks = jnp.stack([y[:, i * width : (i + 1) * width] for i in range(n_narrow)])
    total = None
    for k in range(n_narrow):
        pairs = []
        for h in range(n_narrow):
            for j in range(repeat):
                for n in range(n_narrow):
                    source = (h * repeat + j) * n_narrow + n
                    target = (n * repeat + j) * n_narrow + (h + k) % n_narrow
                    pairs.append((source, target))
        send = lax.dynamic_index_in_dim(blocks, (hi + k) % n_narrow, 0, keepdims=False)
        got = lax.ppermute(send, ("wide", "narrow"), pairs).astype(F32)
        total = got if total is None else total + got
    return total


TILE = 256


def fill_mask(row_ref, col_ref, mask_ref):
    col = col_ref[0]
    row = row_ref[0]
    shape = (BIG, BIG)
    same = (col >> 1) == (row >> 1)
    own = lax.broadcasted_iota(jnp.int32, shape, 0) == lax.broadcasted_iota(jnp.int32, shape, 1)
    usable = jnp.broadcast_to((col & 1) == 1, shape) | own
    mask_ref[...] = jnp.where(same & usable, 0.0, MASKED)


def nn(a, b):
    return lax.dot_general(a, b, (((1,), (0,)), ((), ())), preferred_element_type=F32)


def nt(a, b):
    return lax.dot_general(a, b, (((1,), (1,)), ((), ())), preferred_element_type=F32)


def tn(a, b):
    return lax.dot_general(a, b, (((0,), (0,)), ((), ())), preferred_element_type=F32)


FORWARD_TILE = 512


def forward_kernel(q_ref, k_ref, v_ref, row_ref, col_ref, o_ref, l_ref, mask_ref):
    @pl.when(pl.program_id(1) == 0)
    def _():
        fill_mask(row_ref, col_ref, mask_ref)

    keys = k_ref[0, 0].T
    values = v_ref[0, 0]
    parts = [slice(i, i + FORWARD_TILE) for i in range(0, BIG, FORWARD_TILE)]

    def scores_of(part):
        return nn(keys, q_ref[0, 0, :, part]) * (FACTOR * LOG2E) + mask_ref[:, part]

    following = scores_of(parts[0])
    for place, part in enumerate(parts):
        scores = following
        if place + 1 < len(parts):
            following = scores_of(parts[place + 1])
        top = jnp.max(scores, axis=0, keepdims=True)
        weights = jnp.exp2(scores - top)
        total = jnp.sum(weights, axis=0, keepdims=True)
        mixed = nn(values, weights.astype(BF16))
        o_ref[0, :, part] = (mixed * (1.0 / total)).astype(BF16)
        l_ref[0, :, part] = top + jnp.log2(total)


def backward_kernel(
    q_ref, k_ref, v_ref, g_ref, o_ref, l_ref, row_ref, col_ref, d_ref, mask_ref
):
    @pl.when(pl.program_id(1) == 0)
    def _():
        fill_mask(row_ref, col_ref, mask_ref)

    keys_t = k_ref[0, 0]
    keys = keys_t.T
    values = v_ref[0, 0].T
    key_grad = jnp.zeros((BIG, HEAD), F32)
    value_grad = jnp.zeros((BIG, HEAD), F32)
    parts = [slice(i, i + TILE) for i in range(0, BIG, TILE)]

    def products_of(part):
        return nn(keys, q_ref[0, 0, :, part]), nn(values, g_ref[0, :, part])

    following = products_of(parts[0])
    for place, part in enumerate(parts):
        product, prob_grad = following
        if place + 1 < len(parts):
            following = products_of(parts[place + 1])
        queries = q_ref[0, 0, :, part]
        grads = g_ref[0, :, part]
        delta = jnp.sum(
            grads.astype(F32) * o_ref[0, :, part].astype(F32), axis=0, keepdims=True
        )
        scores = product * (FACTOR * LOG2E) + mask_ref[:, part]
        probs = jnp.exp2(scores - l_ref[0, :, part])
        score_grad = (probs * (prob_grad - delta)).astype(BF16)
        value_grad = value_grad + nt(probs.astype(BF16), grads)
        key_grad = key_grad + nt(score_grad, queries)
        d_ref[0, 0, :, part] = (nn(keys_t, score_grad) * FACTOR).astype(BF16)
    d_ref[1, 0] = (key_grad * FACTOR).T.astype(BF16)
    d_ref[2, 0] = value_grad.T.astype(BF16)


def projected_spec(kind, first=0):
    return pl.BlockSpec((1, 1, HEAD, BIG), lambda c, h: (kind, first + h, 0, c))


def label_operands(labels):
    chunks = labels.shape[0] // BIG
    return labels.reshape(chunks, 1, BIG), labels.reshape(chunks, BIG, 1)


LABEL_SPECS = [
    pl.BlockSpec((1, 1, BIG), lambda c, h: (c, 0, 0)),
    pl.BlockSpec((1, BIG, 1), lambda c, h: (c, 0, 0)),
]
WIDE_SPEC = pl.BlockSpec((1, HEAD, BIG), lambda c, h: (h, 0, c))
LINE_SPEC = pl.BlockSpec((1, 1, BIG), lambda c, h: (h, 0, c))


def attend_forward(projected, labels, first, heads):
    count = projected.shape[3]
    return pl.pallas_call(
        forward_kernel,
        grid=(count // BIG, heads),
        in_specs=[projected_spec(kind, first) for kind in range(3)] + LABEL_SPECS,
        out_specs=[WIDE_SPEC, LINE_SPEC],
        out_shape=[
            jax.ShapeDtypeStruct((heads, HEAD, count), BF16),
            jax.ShapeDtypeStruct((heads, 1, count), F32),
        ],
        scratch_shapes=[pltpu.VMEM((BIG, BIG), F32)],
        name="attend_forward",
    )(projected, projected, projected, *label_operands(labels))


def attend_backward(projected, grads, attended, log_total, labels, first):
    heads = log_total.shape[0]
    count = projected.shape[3]
    return pl.pallas_call(
        backward_kernel,
        grid=(count // BIG, heads),
        in_specs=[projected_spec(kind, first) for kind in range(3)]
        + [pl.BlockSpec((1, HEAD, BIG), lambda c, h: (first + h, 0, c))]
        + [WIDE_SPEC, LINE_SPEC]
        + LABEL_SPECS,
        out_specs=pl.BlockSpec((3, 1, HEAD, BIG), lambda c, h: (0, h, 0, c)),
        out_shape=jax.ShapeDtypeStruct((3, heads, HEAD, count), BF16),
        scratch_shapes=[pltpu.VMEM((BIG, BIG), F32)],
        name="attend_backward",
    )(projected, projected, projected, grads, attended, log_total, *label_operands(labels))


def normalise(values):
    centred = values - jnp.mean(values, axis=-1, keepdims=True)
    scale = lax.rsqrt(jnp.mean(centred * centred, axis=-1, keepdims=True) + EPSILON)
    return centred * scale, scale


def normalise_back(normed, scale, grad):
    return scale * (
        grad
        - jnp.mean(grad, axis=-1, keepdims=True)
        - normed * jnp.mean(grad * normed, axis=-1, keepdims=True)
    )


def row_spec(width, offset=0):
    return pl.BlockSpec((SMALL, width), lambda i: (offset + i, 0))


def piece_spec(piece, width, offset=0):
    return pl.BlockSpec((1, 1, width), lambda i: (offset + i, 0, piece))


def sums_spec(count, width):
    return pl.BlockSpec((1, count, width), lambda i: (i, 0, 0))


def column_sum(values):
    return jnp.sum(values, axis=0, keepdims=True)


def first_kernel(x_ref, shift_ref, scale_ref, *rest):
    normed, _ = normalise(x_ref[...].astype(F32))
    rest[-1][...] = (normed * (1.0 + scale_ref[0]) + shift_ref[0]).T.astype(BF16)


def first_norm(shards, per_block):
    rows, width = shards[0].shape
    blocks = rows // SMALL
    out = None
    for place, shard in enumerate(shards):
        offset = place * blocks
        out = pl.pallas_call(
            first_kernel,
            grid=(blocks,),
            in_specs=[row_spec(width), piece_spec(0, width, offset), piece_spec(1, width, offset)]
            + ([] if out is None else [pl.BlockSpec(memory_space=pl.ANY)]),
            out_specs=pl.BlockSpec((width, SMALL), lambda i, offset=offset: (0, offset + i)),
            out_shape=jax.ShapeDtypeStruct((width, rows * len(shards)), BF16),
            input_output_aliases={} if out is None else {3: 0},
            name="first_norm",
        )(shard, per_block, per_block, *([] if out is None else [out]))
    return out


def second_kernel(count, me_ref, *refs):
    parts = refs[:count]
    weight_ref, bias_ref, gate_ref, shift_ref, scale_ref, x_ref = refs[count : count + 6]
    branch_ref, middle_ref, o_ref, ordered_ref = refs[count + 6 :]
    for place, part_ref in enumerate(parts):
        ordered_ref[((me_ref[0] ^ (place // 2)) * 2) + place % 2] = part_ref[...]
    ordered = ordered_ref[...].reshape(weight_ref.shape[0], SMALL)
    branch = tn(ordered, weight_ref[...]) + bias_ref[...]
    middle = x_ref[...].astype(F32) + gate_ref[0] * branch
    normed, _ = normalise(middle)
    branch_ref[...] = branch
    middle_ref[...] = middle
    o_ref[...] = (normed * (1.0 + scale_ref[0]) + shift_ref[0]).astype(BF16)


def second_norm(parts, me, proj_weight, bias, per_block, tokens_all, rows):
    count, width = tokens_all.shape
    blocks = count // SMALL
    own = rows // SMALL
    features = parts[0].shape[0]
    n_parts = len(parts)

    def turned(i):
        return blocks - 1 - i

    def part_spec(place):
        def index(i, me_ref):
            block = turned(i)
            return (0, ((block // own) ^ (place // 2)) * own + block % own)

        return pl.BlockSpec((features, SMALL), index)

    def piece(kind):
        return pl.BlockSpec((1, 1, width), lambda i, me_ref: (turned(i), 0, kind))

    kept = pl.BlockSpec((SMALL, width), lambda i, me_ref: (jnp.minimum(turned(i), own - 1), 0))
    all_rows = pl.BlockSpec((SMALL, width), lambda i, me_ref: (turned(i), 0))
    return pl.pallas_call(
        functools.partial(second_kernel, n_parts),
        grid_spec=pltpu.PrefetchScalarGridSpec(
            num_scalar_prefetch=1,
            grid=(blocks,),
            in_specs=[part_spec(p) for p in range(n_parts)]
            + [
                pl.BlockSpec((n_parts * features, width), lambda i, me_ref: (0, 0)),
                pl.BlockSpec((1, width), lambda i, me_ref: (0, 0)),
                piece(2),
                piece(3),
                piece(4),
                all_rows,
            ],
            out_specs=[kept, kept, all_rows],
            scratch_shapes=[pltpu.VMEM((n_parts, features, SMALL), BF16)],
        ),
        out_shape=[
            jax.ShapeDtypeStruct((rows, width), F32),
            jax.ShapeDtypeStruct((rows, width), F32),
            jax.ShapeDtypeStruct((count, width), BF16),
        ],
        name="second_norm",
    )(
        me.reshape(1),
        *parts,
        proj_weight,
        bias,
        per_block,
        per_block,
        per_block,
        tokens_all,
    )


def added(refs):
    total = refs[0][...].astype(F32)
    for ref in refs[1:]:
        total = total + ref[...].astype(F32)
    return total


def second_back_kernel(count, *refs):
    middle_ref, branch_ref, g_ref, gate_ref, scale_ref = refs[count : count + 5]
    d_ref, b_ref, s_ref = refs[count + 5 :]
    grad = added(refs[:count])
    normed, ratio = normalise(middle_ref[...])
    total = g_ref[...].astype(F32) + normalise_back(normed, ratio, grad * (1.0 + scale_ref[0]))
    branch_grad = (gate_ref[0] * total).astype(BF16)
    d_ref[...] = total
    b_ref[...] = branch_grad
    s_ref[0] = jnp.concatenate(
        [
            column_sum(total * branch_ref[...]),
            column_sum(grad),
            column_sum(grad * normed),
            column_sum(branch_grad.astype(F32)),
        ],
        axis=0,
    )


def second_back(parts, middle, branch1, output_grad, per_block):
    rows, width = middle.shape
    blocks = rows // SMALL
    return pl.pallas_call(
        functools.partial(second_back_kernel, len(parts)),
        grid=(blocks,),
        in_specs=[row_spec(width)] * (len(parts) + 3)
        + [piece_spec(2, width), piece_spec(4, width)],
        out_specs=[row_spec(width), row_spec(width), sums_spec(4, width)],
        out_shape=[
            jax.ShapeDtypeStruct((rows, width), F32),
            jax.ShapeDtypeStruct((rows, width), BF16),
            jax.ShapeDtypeStruct((blocks, 4, width), F32),
        ],
        name="second_back",
    )(*parts, middle, branch1, output_grad, per_block, per_block)


def output_kernel(count, *refs):
    middle_ref, g_ref, gate_ref, bias_ref, o_ref, s_ref = refs[count:]
    branch = added(refs[:count]) + bias_ref[...]
    grad = g_ref[...].astype(F32)
    o_ref[...] = (middle_ref[...] + gate_ref[0] * branch).astype(BF16)
    s_ref[0] = jnp.concatenate(
        [
            column_sum(grad * branch),
            column_sum((gate_ref[0] * grad).astype(BF16).astype(F32)),
        ],
        axis=0,
    )


def finish_output(parts, middle, output_grad, per_block, bias):
    rows, width = middle.shape
    blocks = rows // SMALL
    return pl.pallas_call(
        functools.partial(output_kernel, len(parts)),
        grid=(blocks,),
        in_specs=[row_spec(width)] * (len(parts) + 2)
        + [piece_spec(5, width), pl.BlockSpec((1, width), lambda i: (0, 0))],
        out_specs=[row_spec(width), sums_spec(2, width)],
        out_shape=[
            jax.ShapeDtypeStruct((rows, width), BF16),
            jax.ShapeDtypeStruct((blocks, 2, width), F32),
        ],
        name="finish_output",
    )(*parts, middle, output_grad, per_block, bias)


def first_sums_kernel(part_ref, x_ref, s_ref):
    grad = part_ref[...].astype(F32)
    normed, _ = normalise(x_ref[...].astype(F32))
    s_ref[0] = jnp.concatenate([column_sum(grad), column_sum(grad * normed)], axis=0)


def first_sums(part, tokens_all):
    count, width = tokens_all.shape
    return pl.pallas_call(
        first_sums_kernel,
        grid=(count // SMALL,),
        in_specs=[row_spec(width)] * 2,
        out_specs=sums_spec(2, width),
        out_shape=jax.ShapeDtypeStruct((count // SMALL, 2, width), F32),
        name="first_sums",
    )(part, tokens_all)


def first_back_kernel(count, *refs):
    x_ref, d_ref, scale_ref, o_ref = refs[count:]
    grad = added(refs[:count])
    normed, ratio = normalise(x_ref[...].astype(F32))
    o_ref[...] = d_ref[...] + normalise_back(normed, ratio, grad * (1.0 + scale_ref[0]))


def first_back(parts, tokens, middle_grad, per_block):
    rows, width = tokens.shape
    return pl.pallas_call(
        functools.partial(first_back_kernel, len(parts)),
        grid=(rows // SMALL,),
        in_specs=[row_spec(width)] * (len(parts) + 2) + [piece_spec(1, width)],
        out_specs=row_spec(width),
        out_shape=jax.ShapeDtypeStruct((rows, width), F32),
        name="first_back",
    )(*parts, tokens, middle_grad, per_block)


def blocked(x):
    return x.reshape(x.shape[0] // SMALL, SMALL, x.shape[1])


def flat(x):
    return x.reshape(x.shape[0] * x.shape[1], x.shape[2])


def turn_kernel(me_ref, w_ref, o_ref, turned_ref):
    turned_ref[...] = w_ref[...].T
    count = o_ref.shape[1]
    o_ref[0] = turned_ref[pl.ds(pl.multiple_of(me_ref[0] * count, 16), count), :]


def turned_weight(weight, me, count):
    width = weight.shape[0]
    depth = width // 3
    return pl.pallas_call(
        turn_kernel,
        grid_spec=pltpu.PrefetchScalarGridSpec(
            num_scalar_prefetch=1,
            grid=(3, 3),
            in_specs=[pl.BlockSpec((depth, width), lambda kind, i, me_ref: (i, kind))],
            out_specs=pl.BlockSpec((1, count, depth), lambda kind, i, me_ref: (kind, 0, i)),
            scratch_shapes=[pltpu.VMEM((width, depth), weight.dtype)],
        ),
        out_shape=jax.ShapeDtypeStruct((3, count, width), weight.dtype),
        name="turned_weight",
    )(me.reshape(1), weight).reshape(3 * count, width)


GELU = math.sqrt(2.0 / math.pi)
CUBIC = 0.044715


def hidden_kernel(me_ref, x_ref, w_ref, bias_ref, g_ref, h_ref, d_ref, s_ref):
    weight = w_ref[...]
    bias = bias_ref[...]
    count = x_ref.shape[0]
    parts = [slice(i, i + SMALL) for i in range(0, count, SMALL)]
    following = nn(x_ref[parts[0], :], weight)
    total = jnp.zeros(bias.shape, F32)
    for place, part in enumerate(parts):
        before = following + bias
        if place + 1 < len(parts):
            following = nn(x_ref[parts[place + 1], :], weight)
        square = before * before
        bent = jnp.tanh(before * (GELU + GELU * CUBIC * square))
        half = 0.5 * before
        raised = 1.0 + bent
        h_ref[part, :] = (half * raised).astype(BF16)
        slope = 0.5 * raised + half * (1.0 - bent * bent) * (GELU + 3.0 * GELU * CUBIC * square)
        grad = (g_ref[part, :].astype(F32) * slope).astype(BF16)
        d_ref[part, :] = grad
        total = total + column_sum(grad.astype(F32))
    s_ref[...] = total


def hidden_and_grad(x, fc1_weight, fc1_mine, bias, hidden_grad, me):
    count, width = x.shape
    columns = hidden_grad.shape[1]
    tile = 256 if columns % 256 == 0 else columns
    tiles = columns // tile
    if tile == columns:
        weight, first = fc1_mine, 0
    else:
        weight, first = fc1_weight, tiles
    block = pl.BlockSpec((count, tile), lambda i, me_ref: (0, i))
    line = pl.BlockSpec((1, tile), lambda i, me_ref: (0, i))
    return pl.pallas_call(
        hidden_kernel,
        grid_spec=pltpu.PrefetchScalarGridSpec(
            num_scalar_prefetch=1,
            grid=(tiles,),
            in_specs=[
                pl.BlockSpec((count, width), lambda i, me_ref: (0, 0)),
                pl.BlockSpec((width, tile), lambda i, me_ref: (0, me_ref[0] * first + i)),
                line,
                block,
            ],
            out_specs=[block, block, line],
        ),
        out_shape=[
            jax.ShapeDtypeStruct((count, columns), BF16),
            jax.ShapeDtypeStruct((count, columns), BF16),
            jax.ShapeDtypeStruct((1, columns), F32),
        ],
        name="hidden_and_grad",
    )(me.reshape(1), x, weight, bias, hidden_grad)


SHARDS = 4


def weight_kernel(core_ref, x_ref, g_ref, keep_ref, send_ref):
    product = nt(x_ref[...], g_ref[...])
    rows = product.shape[0] // SHARDS

    def store(first, second):
        for place in range(SHARDS):
            target = (first, second)[place % 2]
            target[place // 2] = product[place * rows : (place + 1) * rows].astype(BF16)

    @pl.when(core_ref[0] == 0)
    def _():
        store(keep_ref, send_ref)

    @pl.when(core_ref[0] != 0)
    def _():
        store(send_ref, keep_ref)


def weight_halves(turned, grads, wide, n_wide):
    width, count = turned.shape
    rows = width // n_wide
    columns = grads.shape[0]
    block = pl.BlockSpec((SHARDS // 2, rows, columns), lambda i, core: (i, 0, 0))
    shape = jax.ShapeDtypeStruct((n_wide // 2, rows, columns), BF16)
    return pl.pallas_call(
        weight_kernel,
        grid_spec=pltpu.PrefetchScalarGridSpec(
            num_scalar_prefetch=1,
            grid=(n_wide // SHARDS,),
            in_specs=[
                pl.BlockSpec((SHARDS * rows, count), lambda i, core: (i, 0)),
                pl.BlockSpec((columns, count), lambda i, core: (0, 0)),
            ],
            out_specs=[block, block],
        ),
        out_shape=[shape, shape],
        name="weight_halves",
    )((wide & 1).reshape(1), turned, grads)


class Halving:
    def __init__(self, value, bits, n_wide, wide, pair=None):
        self.bits, self.n_wide, self.wide, self.done = bits, n_wide, wide, 0
        self.value = None if value is None else split_bits(value, bits)
        self.pair = pair

    def step(self, anchor, steps=1):
        for _ in range(steps):
            if self.done == self.bits:
                break
            if self.pair is not None:
                keep, send = self.pair
                got = swap(send, "wide", self.n_wide, 1)
                total = after(keep, anchor).astype(F32) + got.astype(F32)
                total = total.astype(BF16)
                self.value = total.reshape((2,) * (self.bits - 1) + total.shape[1:])
                self.pair = None
            else:
                self.value = halve_first(
                    self.value, self.done, self.n_wide, self.wide, anchor
                )
            self.done += 1
        return self.value

    def finish(self, anchor):
        return self.step(anchor, self.bits)


def after(x, *others):
    return lax.optimization_barrier((x,) + others)[0]


def received(others, n_narrow):
    return [
        swap(other, "narrow", n_narrow, j) for j, other in enumerate(others, start=1)
    ]


def row_shards(x, rows, axis):
    return [
        lax.slice_in_dim(x, j * rows, (j + 1) * rows, axis=axis)
        for j in range(x.shape[axis] // rows)
    ]


def shards_of(x, n_narrow):
    out = [x]
    mask = 1
    while mask < n_narrow:
        out = out + [swap(o, "narrow", n_narrow, mask) for o in out]
        mask *= 2
    return out


def body(
    n_wide,
    n_narrow,
    tokens,
    conditions,
    segment_ids,
    pad_mask,
    segment_image,
    ada_weight,
    ada_bias,
    qkv_weight,
    trunk_bias,
    proj_weight,
    fc1_weight,
    fc2_weight,
    output_grad,
):
    rows, width = tokens.shape
    hidden_width = fc1_weight.shape[1]
    me = lax.axis_index("narrow")
    wide = lax.axis_index("wide")
    stages = n_wide.bit_length() - 1
    low_stages = (n_wide // n_narrow).bit_length() - 1
    hi = wide >> low_stages
    heads = HEADS // n_narrow
    half_heads = heads // 2
    head_width = heads * HEAD
    fc_width = hidden_width // n_narrow
    own_blocks = rows // SMALL
    image_count = conditions.shape[0]
    biases = trunk_bias.astype(F32)
    query_bias = biases[:width]
    value_bias = biases[width : 2 * width]
    proj_bias = biases[2 * width : 3 * width][None, :]
    first_bias = biases[3 * width : 3 * width + hidden_width]
    second_bias = biases[3 * width + hidden_width :][None, :]
    mine_of = functools.partial(lax.dynamic_slice_in_dim, axis=0)

    token_shards = shards_of(tokens, n_narrow)
    labels = gather_relative(segment_ids * 2 + pad_mask, "narrow", n_narrow).reshape(-1)
    grad_shards = shards_of(after(output_grad, token_shards[-1]), n_narrow)

    conditions32 = conditions.astype(F32)
    act = jax.nn.silu(conditions32).astype(BF16)
    columns = (
        jnp.dot(act, ada_weight, preferred_element_type=F32) + ada_bias.astype(F32)
    ).astype(BF16)
    modulation = absolute(gather_relative(columns, "narrow", n_narrow), me, n_narrow)
    modulation = modulation.transpose(1, 0, 2).reshape(image_count, -1)
    slots = labels[::SMALL] >> 1
    image = jnp.sum(
        jnp.where(
            slots[:, None] == jnp.arange(image_count, dtype=jnp.int32)[None, :],
            segment_image[0][None, :],
            0,
        ),
        axis=1,
    )
    pick = image[:, None] == jnp.arange(image_count, dtype=jnp.int32)[None, :]
    per_block = jnp.dot(pick.astype(BF16), modulation, preferred_element_type=F32)[:, None, :]

    qkv_turned = turned_weight(qkv_weight, me, head_width)
    qkv_bias = jnp.concatenate(
        [
            mine_of(query_bias, me * head_width, head_width),
            jnp.zeros((head_width,), F32),
            mine_of(value_bias, me * head_width, head_width),
        ]
    )
    first_in_turned = first_norm(token_shards, per_block)
    tokens_all = jnp.concatenate(token_shards, axis=0)
    projected = (nn(qkv_turned, first_in_turned) + qkv_bias[:, None]).astype(BF16)
    projected = projected.reshape(3, heads, HEAD, -1)
    attended0, log_total0 = attend_forward(projected, labels, 0, half_heads)
    attended1, log_total1 = attend_forward(
        after(projected, attended0), labels, half_heads, half_heads
    )
    half_width = half_heads * HEAD
    attended = [attended0.reshape(half_width, -1), attended1.reshape(half_width, -1)]
    gathered = []
    for part in attended:
        gathered.append(shards_of(part, n_narrow))

    fc1_mine = lax.dynamic_slice_in_dim(fc1_weight, me * fc_width, fc_width, axis=1)
    fc2_mine = lax.dynamic_slice_in_dim(fc2_weight, me * fc_width, fc_width, axis=0)
    output_grad_all = after(jnp.concatenate(grad_shards, axis=0), attended1)
    gate2 = per_block[:, :, 5 * width :]
    branch2_grad_all = flat(gate2 * blocked(output_grad_all.astype(F32))).astype(BF16)
    hidden_grad = nt(branch2_grad_all, fc2_mine).astype(BF16)

    branch1, middle, second_in_all = second_norm(
        [gathered[s][j] for j in range(n_narrow) for s in range(2)],
        me,
        proj_weight,
        proj_bias,
        per_block,
        after(tokens_all, hidden_grad),
        rows,
    )

    hidden, before_grad, before_sums = hidden_and_grad(
        second_in_all,
        fc1_weight,
        fc1_mine,
        mine_of(first_bias, me * fc_width, fc_width)[None, :],
        hidden_grad,
        me,
    )
    own_grad, *other_grads = row_shards(before_grad, rows, 0)
    second_in_others = [nt(g, fc1_mine).astype(BF16) for g in other_grads]
    second_in_mine = nt(after(own_grad, *second_in_others), fc1_mine)
    second_in_parts = [second_in_mine] + received(second_in_others, n_narrow)
    fc2_local = tn(after(hidden, second_in_mine), branch2_grad_all).astype(BF16)
    fc1_local = tn(after(second_in_all, fc2_local), before_grad).astype(BF16)

    fc2_sum = Halving(fc2_local, low_stages, n_wide, wide)
    fc1_sum = Halving(fc1_local, stages, n_wide, wide)
    tied = fc2_sum.step(fc1_local)

    middle_grad, branch1_grad, second_sums = second_back(
        second_in_parts, after(middle, tied), branch1, output_grad, per_block
    )
    branch1_grad_all = jnp.concatenate(shards_of(branch1_grad, n_narrow), axis=0)
    own_hidden, *other_hidden = row_shards(after(hidden, branch1_grad), rows, 0)
    branch2_others = [nn(h, fc2_mine).astype(BF16) for h in other_hidden]
    branch2_mine = nn(own_hidden, fc2_mine)
    tied = fc1_sum.step((branch2_mine, branch2_others))
    branch1_grad_all = after(branch1_grad_all, tied)
    proj_mine = lax.dynamic_slice_in_dim(proj_weight, me * head_width, head_width, axis=0)
    attended_grad = nt(proj_mine, branch1_grad_all).astype(BF16).reshape(heads, HEAD, -1)
    projected_grad0 = attend_backward(projected, attended_grad, attended0, log_total0, labels, 0)
    branch2_parts = [branch2_mine] + received(
        [after(b, branch1_grad_all) for b in branch2_others], n_narrow
    )
    tied = fc2_sum.step(projected_grad0)
    grad0 = projected_grad0.reshape(3 * half_width, -1)
    qkv0_pair = weight_halves(first_in_turned, after(grad0, tied), wide, n_wide)
    qkv0_sum = Halving(None, stages, n_wide, wide, qkv0_pair)
    proj_local = jnp.concatenate(
        [nn(after(a, qkv0_pair[0]), branch1_grad_all).astype(BF16) for a in attended], axis=0
    )
    proj_sum = Halving(proj_local, low_stages, n_wide, wide)
    output, output_sums = finish_output(
        branch2_parts,
        middle,
        after(output_grad, proj_local),
        per_block,
        second_bias,
    )
    tied = fc1_sum.step(output)

    def put(size, part):
        return lax.dynamic_update_slice_in_dim(
            jnp.zeros((size,), F32), part, me * part.shape[0], axis=0
        )

    def put_half(part):
        return put(width, jnp.concatenate([part, jnp.zeros((half_width,), F32)]))

    bias_local = jnp.concatenate(
        [
            put_half(jnp.sum(grad0[:half_width].astype(F32), axis=1)),
            put_half(jnp.sum(grad0[2 * half_width :].astype(F32), axis=1)),
            jnp.sum(second_sums[:, 3], axis=0),
            put(hidden_width, before_sums[0]),
            jnp.sum(output_sums[:, 1], axis=0),
        ]
    )
    bias_width = bias_local.shape[0] // (n_wide * n_narrow)
    bias_local = bias_local.reshape(n_wide, n_narrow, bias_width).transpose(1, 0, 2)
    bias_local = bias_local.reshape(n_narrow, image_count, -1)
    projected_grad1 = attend_backward(
        projected,
        after(attended_grad, tied, proj_sum.step(output), bias_local),
        attended1,
        log_total1,
        labels,
        half_heads,
    )
    grad1 = projected_grad1.reshape(3 * half_width, -1)

    tied = qkv0_sum.step(projected_grad1)
    projected_grad = jnp.concatenate([projected_grad0, projected_grad1], axis=1)
    projected_grad = after(projected_grad.reshape(3 * head_width, -1), tied)
    grad_shards1 = row_shards(projected_grad, rows, 1)
    first_in_others = [tn(g, qkv_turned).astype(BF16) for g in grad_shards1[1:]]
    first_in_arrived = received(first_in_others, n_narrow)
    qkv1_pair = weight_halves(
        first_in_turned, after(grad1, *first_in_others), wide, n_wide
    )
    qkv1_sum = Halving(None, stages, n_wide, wide, qkv1_pair)
    own_grads = after(grad_shards1[0], qkv1_pair[0])
    first_in_mine = tn(own_grads, qkv_turned)
    tied = (qkv1_sum.step(first_in_mine), fc2_sum.step(first_in_mine))

    first_block_sums = [
        first_sums(after(g, tied), x)
        for g, x in zip([first_in_mine] + first_in_others, token_shards)
    ]
    first_block_sums = jnp.concatenate(first_block_sums, axis=0)
    tied = qkv0_sum.step(first_block_sums)

    def by_image(choice, sums):
        return lax.dot_general(
            choice.astype(F32),
            sums.reshape(sums.shape[0], -1),
            (((0,), (0,)), ((), ())),
            precision=lax.Precision.HIGHEST,
            preferred_element_type=F32,
        )

    modulation_part = jnp.concatenate(
        [
            by_image(pick, first_block_sums),
            by_image(pick[:own_blocks], second_sums[:, :3]),
            by_image(pick[:own_blocks], output_sums[:, :1]),
        ],
        axis=1,
    )
    modulation_part = modulation_part.reshape(image_count, n_narrow, -1).transpose(1, 0, 2)

    per_row = n_wide // image_count
    shape = (n_narrow, image_count, per_row * bias_width)
    owner = lax.broadcasted_iota(jnp.int32, shape, 0)
    row = lax.broadcasted_iota(jnp.int32, shape, 1)
    column = lax.broadcasted_iota(jnp.int32, shape, 2) // bias_width
    place = (row * per_row + column) * n_narrow + owner
    for first, base in ((0, 0), (2 * half_width, width)):
        sums = jnp.sum(grad1[first : first + half_width].astype(F32), axis=1)
        start = (base + me * head_width + half_width) // bias_width
        for k in range(half_width // bias_width):
            line = jnp.tile(sums[k * bias_width : (k + 1) * bias_width], per_row)
            bias_local = bias_local + jnp.where(place == start + k, line[None, None, :], 0.0)
    small = jnp.concatenate([modulation_part, bias_local], axis=2)
    relative = absolute(small, me, n_narrow)
    small = scatter_relative(
        relative[0], [relative[j] for j in range(1, n_narrow)], "narrow", n_narrow
    ).astype(BF16)
    tokens_grad = first_back(
        [first_in_mine] + first_in_arrived,
        tokens,
        after(middle_grad, relative, qkv0_sum.value),
        per_block,
    )
    column_count = small.shape[1] - n_wide * bias_width // image_count
    modulation_grad = small[:, :column_count]
    together = jnp.concatenate([small, act], axis=1)[None]
    tied = qkv1_sum.step(tokens_grad)
    plan = [
        lambda anchor: (qkv0_sum.step(anchor), proj_sum.step(anchor), fc1_sum.step(anchor)),
        lambda anchor: (qkv1_sum.step(anchor),),
        lambda anchor: (qkv0_sum.step(anchor), proj_sum.step(anchor), fc1_sum.step(anchor)),
        lambda anchor: (qkv1_sum.step(anchor),),
    ]
    for stage in range(stages):
        arrived = swap(together, "wide", n_wide, n_wide >> (stage + 1))
        together = jnp.concatenate([after(together, tied), arrived], axis=0)
        if stage == 1:
            modulation_grad = after(modulation_grad, together)
        if stage < len(plan):
            tied = plan[stage](together)
    qkv0_sum.finish(together)
    qkv1_sum.finish(together)
    fc1_sum.finish(together)
    proj_sum.finish(together)
    bias_sum = jnp.sum(together[:, :, column_count:-width].astype(F32), axis=0)
    bias_sum = lax.dynamic_index_in_dim(
        bias_sum.reshape(n_wide, bias_width), wide, 0, keepdims=False
    )
    together = after(together, qkv1_sum.value).reshape(n_wide * image_count, -1)
    modulation_grad_all = together[:, :column_count]
    ada_weight_grad = tn(together[:, -width:], modulation_grad_all)
    ada_bias_grad = jnp.sum(modulation_grad_all.astype(F32), axis=0)

    proj_flat = rows_to_columns(proj_sum.value, n_wide, n_narrow, hi)
    fc2_flat = rows_to_columns(fc2_sum.finish(output), n_wide, n_narrow, hi)
    fc1_flat = fc1_sum.value.astype(F32)
    qkv_sum = jnp.stack([qkv0_sum.value, qkv1_sum.value]).reshape(2, -1, 3, half_width)
    qkv_all = absolute(gather_relative(qkv_sum, "narrow", n_narrow), me, n_narrow)
    qkv_all = qkv_all.transpose(2, 3, 0, 1, 4).reshape(qkv_sum.shape[1], 3 * width)
    qkv_block = 3 * width // n_narrow
    qkv_flat = lax.dynamic_slice_in_dim(qkv_all, me * qkv_block, qkv_block, axis=1)

    act_part = nt(modulation_grad, ada_weight)
    act_part = act_part.reshape(image_count, n_narrow, -1).transpose(1, 0, 2)
    relative = absolute(act_part, me, n_narrow)
    act_grad = scatter_relative(
        relative[0], [relative[j] for j in range(1, n_narrow)], "narrow", n_narrow
    )
    column_width = width // n_narrow
    condition_mine = lax.dynamic_slice_in_dim(conditions32, me * column_width, column_width, 1)
    gate = 1.0 / (1.0 + jnp.exp(-condition_mine))
    conditions_grad = act_grad * (gate * (1.0 + condition_mine * (1.0 - gate)))

    return (
        output,
        tokens_grad,
        conditions_grad,
        ada_weight_grad,
        ada_bias_grad,
        qkv_flat.astype(F32).reshape(1, -1),
        bias_sum.reshape(-1),
        proj_flat.reshape(1, -1),
        fc1_flat.reshape(1, -1),
        fc2_flat.reshape(1, -1),
    )


def solution(mesh):
    placed = (
        P(("wide", "narrow"), None),
        P("wide", None),
        P(("wide", "narrow")),
        P(("wide", "narrow")),
        P("wide", None),
        P(None, "narrow"),
        P("narrow"),
        P(),
        P(),
        P(),
        P(),
        P(),
        P(("wide", "narrow"), None),
    )
    return jax.shard_map(
        functools.partial(body, mesh.shape["wide"], mesh.shape["narrow"]),
        mesh=mesh,
        in_specs=placed,
        out_specs=(
            P(("wide", "narrow"), None),
            P(("wide", "narrow"), None),
            P("wide", "narrow"),
            P(None, "narrow"),
            P("narrow"),
            P("narrow", "wide"),
            P(("wide", "narrow")),
            P("narrow", "wide"),
            P("narrow", "wide"),
            P("narrow", "wide"),
        ),
        check_vma=False,
    )
```

```python
import functools
import math

import jax
import jax.numpy as jnp
from jax import lax
from jax.experimental import pallas as pl
from jax.experimental.pallas import tpu as pltpu
from jax.sharding import PartitionSpec as P


HEADS = 16
HEAD = 72
BIG = 1024
SMALL = 256
EPSILON = 1e-06
MASKED = -1e30
FACTOR = HEAD ** (-0.5)
LOG2E = math.log2(math.e)
BF16 = jnp.bfloat16
F32 = jnp.float32


def swap(x, axis, size, mask):
    return lax.ppermute(x, axis, [(i, i ^ mask) for i in range(size)])


def gather_relative(x, axis, size):
    out = x[None]
    mask = 1
    while mask < size:
        out = jnp.concatenate([out, swap(out, axis, size, mask)], axis=0)
        mask *= 2
    return out


def scatter_relative(mine, others, axis, size):
    total = mine.astype(F32)
    for j in range(1, size):
        total = total + swap(others[j - 1].astype(BF16), axis, size, j).astype(F32)
    return total


def absolute(blocks, me, size):
    if size == 2:
        return jnp.where(me == 0, blocks, blocks[::-1])
    return jnp.take(blocks, jnp.arange(size) ^ me, axis=0)


def halve(y, place, bit, axis, size, index, kind, anchor=None):
    mine = (index >> bit) & 1
    keep = y if anchor is None else after(y, anchor)
    keep = lax.dynamic_index_in_dim(keep, mine, place, keepdims=False)
    send = lax.dynamic_index_in_dim(y, 1 - mine, place, keepdims=False)
    got = swap(send.astype(kind), axis, size, 1 << bit)
    return (keep.astype(F32) + got.astype(F32)).astype(kind)


def split_bits(y, count):
    return y.reshape((2,) * count + (y.shape[0] >> count,) + y.shape[1:])


def halve_first(y, bit, n_wide, wide, anchor):
    return halve(y, y.ndim - 3, bit, "wide", n_wide, wide, BF16, anchor)


def rows_to_columns(y, n_wide, n_narrow, hi, anchor):
    repeat = n_wide // n_narrow
    width = y.shape[1] // n_narrow
    blocks = jnp.stack([y[:, i * width : (i + 1) * width] for i in range(n_narrow)])
    total = None
    for k in range(n_narrow):
        pairs = []
        for h in range(n_narrow):
            for j in range(repeat):
                for n in range(n_narrow):
                    source = (h * repeat + j) * n_narrow + n
                    target = (n * repeat + j) * n_narrow + (h + k) % n_narrow
                    pairs.append((source, target))
        send = lax.dynamic_index_in_dim(blocks, (hi + k) % n_narrow, 0, keepdims=False)
        got = lax.ppermute(send, ("wide", "narrow"), pairs)
        got = lax.optimization_barrier((got, anchor))[0].astype(F32)
        total = got if total is None else total + got
    return total


TILE = 256


def fill_mask(row_ref, col_ref, mask_ref):
    col = col_ref[0]
    row = row_ref[0]
    shape = (BIG, BIG)
    same = (col >> 1) == (row >> 1)
    own = lax.broadcasted_iota(jnp.int32, shape, 0) == lax.broadcasted_iota(jnp.int32, shape, 1)
    usable = jnp.broadcast_to((col & 1) == 1, shape) | own
    mask_ref[...] = jnp.where(same & usable, 0.0, MASKED)


def nn(a, b):
    return lax.dot_general(a, b, (((1,), (0,)), ((), ())), preferred_element_type=F32)


def nt(a, b):
    return lax.dot_general(a, b, (((1,), (1,)), ((), ())), preferred_element_type=F32)


def tn(a, b):
    return lax.dot_general(a, b, (((0,), (0,)), ((), ())), preferred_element_type=F32)


FORWARD_TILE = 512


def forward_kernel(q_ref, k_ref, v_ref, row_ref, col_ref, o_ref, l_ref, mask_ref):
    @pl.when(pl.program_id(1) == 0)
    def _():
        fill_mask(row_ref, col_ref, mask_ref)

    keys = k_ref[0, 0].T
    values = v_ref[0, 0]
    parts = [slice(i, i + FORWARD_TILE) for i in range(0, BIG, FORWARD_TILE)]

    def scores_of(part):
        return nn(keys, q_ref[0, 0, :, part]) * (FACTOR * LOG2E) + mask_ref[:, part]

    following = scores_of(parts[0])
    for place, part in enumerate(parts):
        scores = following
        if place + 1 < len(parts):
            following = scores_of(parts[place + 1])
        top = jnp.max(scores, axis=0, keepdims=True)
        weights = jnp.exp2(scores - top)
        total = jnp.sum(weights, axis=0, keepdims=True)
        mixed = nn(values, weights.astype(BF16))
        o_ref[0, :, part] = (mixed * (1.0 / total)).astype(BF16)
        l_ref[0, :, part] = top + jnp.log2(total)


def backward_kernel(
    q_ref, k_ref, v_ref, g_ref, o_ref, l_ref, row_ref, col_ref, d_ref, mask_ref
):
    @pl.when(pl.program_id(1) == 0)
    def _():
        fill_mask(row_ref, col_ref, mask_ref)

    keys_t = k_ref[0, 0]
    keys = keys_t.T
    values = v_ref[0, 0].T
    key_grad = jnp.zeros((BIG, HEAD), F32)
    value_grad = jnp.zeros((BIG, HEAD), F32)
    parts = [slice(i, i + TILE) for i in range(0, BIG, TILE)]

    def products_of(part):
        return nn(keys, q_ref[0, 0, :, part]), nn(values, g_ref[0, :, part])

    following = products_of(parts[0])
    for place, part in enumerate(parts):
        product, prob_grad = following
        if place + 1 < len(parts):
            following = products_of(parts[place + 1])
        queries = q_ref[0, 0, :, part]
        grads = g_ref[0, :, part]
        delta = jnp.sum(
            grads.astype(F32) * o_ref[0, :, part].astype(F32), axis=0, keepdims=True
        )
        scores = product * (FACTOR * LOG2E) + mask_ref[:, part]
        probs = jnp.exp2(scores - l_ref[0, :, part])
        score_grad = (probs * (prob_grad - delta)).astype(BF16)
        value_grad = value_grad + nt(probs.astype(BF16), grads)
        key_grad = key_grad + nt(score_grad, queries)
        d_ref[0, 0, :, part] = (nn(keys_t, score_grad) * FACTOR).astype(BF16)
    d_ref[1, 0] = (key_grad * FACTOR).T.astype(BF16)
    d_ref[2, 0] = value_grad.T.astype(BF16)


def projected_spec(kind, first=0):
    return pl.BlockSpec((1, 1, HEAD, BIG), lambda c, h: (kind, first + h, 0, c))


def label_operands(labels):
    chunks = labels.shape[0] // BIG
    return labels.reshape(chunks, 1, BIG), labels.reshape(chunks, BIG, 1)


LABEL_SPECS = [
    pl.BlockSpec((1, 1, BIG), lambda c, h: (c, 0, 0)),
    pl.BlockSpec((1, BIG, 1), lambda c, h: (c, 0, 0)),
]
WIDE_SPEC = pl.BlockSpec((1, HEAD, BIG), lambda c, h: (h, 0, c))
LINE_SPEC = pl.BlockSpec((1, 1, BIG), lambda c, h: (h, 0, c))


def attend_forward(projected, labels, first, heads):
    count = projected.shape[3]
    return pl.pallas_call(
        forward_kernel,
        grid=(count // BIG, heads),
        in_specs=[projected_spec(kind, first) for kind in range(3)] + LABEL_SPECS,
        out_specs=[WIDE_SPEC, LINE_SPEC],
        out_shape=[
            jax.ShapeDtypeStruct((heads, HEAD, count), BF16),
            jax.ShapeDtypeStruct((heads, 1, count), F32),
        ],
        scratch_shapes=[pltpu.VMEM((BIG, BIG), F32)],
        name="attend_forward",
    )(projected, projected, projected, *label_operands(labels))


def attend_backward(projected, grads, attended, log_total, labels, first):
    heads = log_total.shape[0]
    count = projected.shape[3]
    return pl.pallas_call(
        backward_kernel,
        grid=(count // BIG, heads),
        in_specs=[projected_spec(kind, first) for kind in range(3)]
        + [pl.BlockSpec((1, HEAD, BIG), lambda c, h: (first + h, 0, c))]
        + [WIDE_SPEC, LINE_SPEC]
        + LABEL_SPECS,
        out_specs=pl.BlockSpec((3, 1, HEAD, BIG), lambda c, h: (0, h, 0, c)),
        out_shape=jax.ShapeDtypeStruct((3, heads, HEAD, count), BF16),
        scratch_shapes=[pltpu.VMEM((BIG, BIG), F32)],
        name="attend_backward",
    )(projected, projected, projected, grads, attended, log_total, *label_operands(labels))


def normalise(values):
    centred = values - jnp.mean(values, axis=-1, keepdims=True)
    scale = lax.rsqrt(jnp.mean(centred * centred, axis=-1, keepdims=True) + EPSILON)
    return centred * scale, scale


def normalise_back(normed, scale, grad):
    return scale * (
        grad
        - jnp.mean(grad, axis=-1, keepdims=True)
        - normed * jnp.mean(grad * normed, axis=-1, keepdims=True)
    )


def row_spec(width, offset=0):
    return pl.BlockSpec((SMALL, width), lambda i: (offset + i, 0))


def piece_spec(piece, width, offset=0):
    return pl.BlockSpec((1, 1, width), lambda i: (offset + i, 0, piece))


def sums_spec(count, width):
    return pl.BlockSpec((1, count, width), lambda i: (i, 0, 0))


def column_sum(values):
    return jnp.sum(values, axis=0, keepdims=True)


def first_kernel(x_ref, shift_ref, scale_ref, *rest):
    normed, _ = normalise(x_ref[...].astype(F32))
    rest[-1][...] = (normed * (1.0 + scale_ref[0]) + shift_ref[0]).T.astype(BF16)


def first_norm(shards, per_block):
    rows, width = shards[0].shape
    blocks = rows // SMALL
    out = None
    for place, shard in enumerate(shards):
        offset = place * blocks
        out = pl.pallas_call(
            first_kernel,
            grid=(blocks,),
            in_specs=[row_spec(width), piece_spec(0, width, offset), piece_spec(1, width, offset)]
            + ([] if out is None else [pl.BlockSpec(memory_space=pl.ANY)]),
            out_specs=pl.BlockSpec((width, SMALL), lambda i, offset=offset: (0, offset + i)),
            out_shape=jax.ShapeDtypeStruct((width, rows * len(shards)), BF16),
            input_output_aliases={} if out is None else {3: 0},
            name="first_norm",
        )(shard, per_block, per_block, *([] if out is None else [out]))
    return out


def second_kernel(count, me_ref, *refs):
    parts = refs[:count]
    weight_ref, bias_ref, gate_ref, shift_ref, scale_ref, x_ref = refs[count : count + 6]
    branch_ref, middle_ref, o_ref, ordered_ref = refs[count + 6 :]
    for place, part_ref in enumerate(parts):
        ordered_ref[((me_ref[0] ^ (place // 2)) * 2) + place % 2] = part_ref[...]
    ordered = ordered_ref[...].reshape(weight_ref.shape[0], SMALL)
    branch = tn(ordered, weight_ref[...]) + bias_ref[...]
    middle = x_ref[...].astype(F32) + gate_ref[0] * branch
    normed, _ = normalise(middle)
    branch_ref[...] = branch
    middle_ref[...] = middle
    o_ref[...] = (normed * (1.0 + scale_ref[0]) + shift_ref[0]).astype(BF16)


def second_norm(parts, me, proj_weight, bias, per_block, tokens_all, rows):
    count, width = tokens_all.shape
    blocks = count // SMALL
    own = rows // SMALL
    features = parts[0].shape[0]
    n_parts = len(parts)

    def turned(i):
        return blocks - 1 - i

    def part_spec(place):
        def index(i, me_ref):
            block = turned(i)
            return (0, ((block // own) ^ (place // 2)) * own + block % own)

        return pl.BlockSpec((features, SMALL), index)

    def piece(kind):
        return pl.BlockSpec((1, 1, width), lambda i, me_ref: (turned(i), 0, kind))

    kept = pl.BlockSpec((SMALL, width), lambda i, me_ref: (jnp.minimum(turned(i), own - 1), 0))
    all_rows = pl.BlockSpec((SMALL, width), lambda i, me_ref: (turned(i), 0))
    return pl.pallas_call(
        functools.partial(second_kernel, n_parts),
        grid_spec=pltpu.PrefetchScalarGridSpec(
            num_scalar_prefetch=1,
            grid=(blocks,),
            in_specs=[part_spec(p) for p in range(n_parts)]
            + [
                pl.BlockSpec((n_parts * features, width), lambda i, me_ref: (0, 0)),
                pl.BlockSpec((1, width), lambda i, me_ref: (0, 0)),
                piece(2),
                piece(3),
                piece(4),
                all_rows,
            ],
            out_specs=[kept, kept, all_rows],
            scratch_shapes=[pltpu.VMEM((n_parts, features, SMALL), BF16)],
        ),
        out_shape=[
            jax.ShapeDtypeStruct((rows, width), F32),
            jax.ShapeDtypeStruct((rows, width), F32),
            jax.ShapeDtypeStruct((count, width), BF16),
        ],
        name="second_norm",
    )(
        me.reshape(1),
        *parts,
        proj_weight,
        bias,
        per_block,
        per_block,
        per_block,
        tokens_all,
    )


def added(refs):
    total = refs[0][...].astype(F32)
    for ref in refs[1:]:
        total = total + ref[...].astype(F32)
    return total


def second_back_kernel(count, *refs):
    middle_ref, branch_ref, g_ref, gate_ref, scale_ref = refs[count : count + 5]
    d_ref, b_ref, s_ref = refs[count + 5 :]
    grad = added(refs[:count])
    normed, ratio = normalise(middle_ref[...])
    total = g_ref[...].astype(F32) + normalise_back(normed, ratio, grad * (1.0 + scale_ref[0]))
    branch_grad = (gate_ref[0] * total).astype(BF16)
    d_ref[...] = total
    b_ref[...] = branch_grad
    s_ref[0] = jnp.concatenate(
        [
            column_sum(total * branch_ref[...]),
            column_sum(grad),
            column_sum(grad * normed),
            column_sum(branch_grad.astype(F32)),
        ],
        axis=0,
    )


def second_back(parts, middle, branch1, output_grad, per_block):
    rows, width = middle.shape
    blocks = rows // SMALL
    return pl.pallas_call(
        functools.partial(second_back_kernel, len(parts)),
        grid=(blocks,),
        in_specs=[row_spec(width)] * (len(parts) + 3)
        + [piece_spec(2, width), piece_spec(4, width)],
        out_specs=[row_spec(width), row_spec(width), sums_spec(4, width)],
        out_shape=[
            jax.ShapeDtypeStruct((rows, width), F32),
            jax.ShapeDtypeStruct((rows, width), BF16),
            jax.ShapeDtypeStruct((blocks, 4, width), F32),
        ],
        name="second_back",
    )(*parts, middle, branch1, output_grad, per_block, per_block)


def output_kernel(count, *refs):
    middle_ref, g_ref, gate_ref, bias_ref, o_ref, s_ref = refs[count:]
    branch = added(refs[:count]) + bias_ref[...]
    grad = g_ref[...].astype(F32)
    o_ref[...] = (middle_ref[...] + gate_ref[0] * branch).astype(BF16)
    s_ref[0] = jnp.concatenate(
        [
            column_sum(grad * branch),
            column_sum((gate_ref[0] * grad).astype(BF16).astype(F32)),
        ],
        axis=0,
    )


def finish_output(parts, middle, output_grad, per_block, bias):
    rows, width = middle.shape
    blocks = rows // SMALL
    return pl.pallas_call(
        functools.partial(output_kernel, len(parts)),
        grid=(blocks,),
        in_specs=[row_spec(width)] * (len(parts) + 2)
        + [piece_spec(5, width), pl.BlockSpec((1, width), lambda i: (0, 0))],
        out_specs=[row_spec(width), sums_spec(2, width)],
        out_shape=[
            jax.ShapeDtypeStruct((rows, width), BF16),
            jax.ShapeDtypeStruct((blocks, 2, width), F32),
        ],
        name="finish_output",
    )(*parts, middle, output_grad, per_block, bias)


def first_sums_kernel(count, *refs):
    sums = []
    for part_ref, x_ref in zip(refs[:count], refs[count : 2 * count]):
        grad = part_ref[...].astype(F32)
        normed, _ = normalise(x_ref[...].astype(F32))
        sums += [column_sum(grad), column_sum(grad * normed)]
    refs[-1][0] = jnp.concatenate(sums, axis=0)


def first_sums(parts, shards):
    rows, width = shards[0].shape
    count = len(parts)
    blocks = rows // SMALL
    sums = pl.pallas_call(
        functools.partial(first_sums_kernel, count),
        grid=(blocks,),
        in_specs=[row_spec(width)] * (2 * count),
        out_specs=sums_spec(2 * count, width),
        out_shape=jax.ShapeDtypeStruct((blocks, 2 * count, width), F32),
        name="first_sums",
    )(*parts, *shards)
    sums = sums.reshape(blocks, count, 2, width).transpose(1, 0, 2, 3)
    return sums.reshape(blocks * count, 2, width)


def first_back_kernel(count, *refs):
    x_ref, d_ref, scale_ref, o_ref = refs[count:]
    grad = added(refs[:count])
    normed, ratio = normalise(x_ref[...].astype(F32))
    o_ref[...] = d_ref[...] + normalise_back(normed, ratio, grad * (1.0 + scale_ref[0]))


def first_back(parts, tokens, middle_grad, per_block):
    rows, width = tokens.shape
    return pl.pallas_call(
        functools.partial(first_back_kernel, len(parts)),
        grid=(rows // SMALL,),
        in_specs=[row_spec(width)] * (len(parts) + 2) + [piece_spec(1, width)],
        out_specs=row_spec(width),
        out_shape=jax.ShapeDtypeStruct((rows, width), F32),
        name="first_back",
    )(*parts, tokens, middle_grad, per_block)


def blocked(x):
    return x.reshape(x.shape[0] // SMALL, SMALL, x.shape[1])


def flat(x):
    return x.reshape(x.shape[0] * x.shape[1], x.shape[2])


def turn_kernel(me_ref, w_ref, o_ref, turned_ref):
    turned_ref[...] = w_ref[...].T
    count = o_ref.shape[1]
    o_ref[0] = turned_ref[pl.ds(pl.multiple_of(me_ref[0] * count, 16), count), :]


def turned_weight(weight, me, count):
    width = weight.shape[0]
    depth = width // 3
    return pl.pallas_call(
        turn_kernel,
        grid_spec=pltpu.PrefetchScalarGridSpec(
            num_scalar_prefetch=1,
            grid=(3, 3),
            in_specs=[pl.BlockSpec((depth, width), lambda kind, i, me_ref: (i, kind))],
            out_specs=pl.BlockSpec((1, count, depth), lambda kind, i, me_ref: (kind, 0, i)),
            scratch_shapes=[pltpu.VMEM((width, depth), weight.dtype)],
        ),
        out_shape=jax.ShapeDtypeStruct((3, count, width), weight.dtype),
        name="turned_weight",
    )(me.reshape(1), weight).reshape(3 * count, width)


GELU = math.sqrt(2.0 / math.pi)
CUBIC = 0.044715


def hidden_kernel(me_ref, x_ref, w_ref, bias_ref, g_ref, h_ref, d_ref, s_ref):
    weight = w_ref[...]
    bias = bias_ref[...]
    count = x_ref.shape[0]
    parts = [slice(i, i + SMALL) for i in range(0, count, SMALL)]
    following = nn(x_ref[parts[0], :], weight)
    total = jnp.zeros(bias.shape, F32)
    for place, part in enumerate(parts):
        before = following + bias
        if place + 1 < len(parts):
            following = nn(x_ref[parts[place + 1], :], weight)
        square = before * before
        power = before * (-2.0 * LOG2E * GELU - 2.0 * LOG2E * GELU * CUBIC * square)
        share = 1.0 / (1.0 + jnp.exp2(power))
        hidden = before * share
        h_ref[part, :] = hidden.astype(BF16)
        slope = share + hidden * (1.0 - share) * (2.0 * GELU + 6.0 * GELU * CUBIC * square)
        grad = (g_ref[part, :].astype(F32) * slope).astype(BF16)
        d_ref[part, :] = grad
        total = total + column_sum(grad.astype(F32))
    s_ref[...] = total


def hidden_and_grad(x, fc1_weight, fc1_mine, bias, hidden_grad, me):
    count, width = x.shape
    columns = hidden_grad.shape[1]
    tile = 256 if columns % 256 == 0 else columns
    tiles = columns // tile
    if tile == columns:
        weight, first = fc1_mine, 0
    else:
        weight, first = fc1_weight, tiles
    block = pl.BlockSpec((count, tile), lambda i, me_ref: (0, i))
    line = pl.BlockSpec((1, tile), lambda i, me_ref: (0, i))
    return pl.pallas_call(
        hidden_kernel,
        grid_spec=pltpu.PrefetchScalarGridSpec(
            num_scalar_prefetch=1,
            grid=(tiles,),
            in_specs=[
                pl.BlockSpec((count, width), lambda i, me_ref: (0, 0)),
                pl.BlockSpec((width, tile), lambda i, me_ref: (0, me_ref[0] * first + i)),
                line,
                block,
            ],
            out_specs=[block, block, line],
        ),
        out_shape=[
            jax.ShapeDtypeStruct((count, columns), BF16),
            jax.ShapeDtypeStruct((count, columns), BF16),
            jax.ShapeDtypeStruct((1, columns), F32),
        ],
        name="hidden_and_grad",
    )(me.reshape(1), x, weight, bias, hidden_grad)


SHARDS = 4


def weight_kernel(core_ref, x_ref, g_ref, keep_ref, send_ref):
    product = nt(x_ref[...], g_ref[...])
    rows = product.shape[0] // SHARDS

    def store(first, second):
        for place in range(SHARDS):
            target = (first, second)[place % 2]
            target[place // 2] = product[place * rows : (place + 1) * rows].astype(BF16)

    @pl.when(core_ref[0] == 0)
    def _():
        store(keep_ref, send_ref)

    @pl.when(core_ref[0] != 0)
    def _():
        store(send_ref, keep_ref)


def weight_halves(turned, grads, wide, n_wide):
    width, count = turned.shape
    rows = width // n_wide
    columns = grads.shape[0]
    block = pl.BlockSpec((SHARDS // 2, rows, columns), lambda i, core: (i, 0, 0))
    shape = jax.ShapeDtypeStruct((n_wide // 2, rows, columns), BF16)
    return pl.pallas_call(
        weight_kernel,
        grid_spec=pltpu.PrefetchScalarGridSpec(
            num_scalar_prefetch=1,
            grid=(n_wide // SHARDS,),
            in_specs=[
                pl.BlockSpec((SHARDS * rows, count), lambda i, core: (i, 0)),
                pl.BlockSpec((columns, count), lambda i, core: (0, 0)),
            ],
            out_specs=[block, block],
        ),
        out_shape=[shape, shape],
        name="weight_halves",
    )((wide & 1).reshape(1), turned, grads)


class Halving:
    def __init__(self, value, bits, n_wide, wide, pair=None):
        self.bits, self.n_wide, self.wide, self.done = bits, n_wide, wide, 0
        self.value = None if value is None else split_bits(value, bits)
        self.pair = pair

    def step(self, anchor, steps=1):
        for _ in range(steps):
            if self.done == self.bits:
                break
            if self.pair is not None:
                keep, send = self.pair
                got = swap(send, "wide", self.n_wide, 1)
                total = after(keep, anchor).astype(F32) + got.astype(F32)
                total = total.astype(BF16)
                self.value = total.reshape((2,) * (self.bits - 1) + total.shape[1:])
                self.pair = None
            else:
                self.value = halve_first(
                    self.value, self.done, self.n_wide, self.wide, anchor
                )
            self.done += 1
        return self.value

    def finish(self, anchor):
        return self.step(anchor, self.bits)


def after(x, *others):
    return lax.optimization_barrier((x,) + others)[0]


def received(others, n_narrow):
    return [
        swap(other, "narrow", n_narrow, j) for j, other in enumerate(others, start=1)
    ]


def row_shards(x, rows, axis):
    return [
        lax.slice_in_dim(x, j * rows, (j + 1) * rows, axis=axis)
        for j in range(x.shape[axis] // rows)
    ]


def shards_of(x, n_narrow):
    out = [x]
    mask = 1
    while mask < n_narrow:
        out = out + [swap(o, "narrow", n_narrow, mask) for o in out]
        mask *= 2
    return out


def body(
    n_wide,
    n_narrow,
    tokens,
    conditions,
    segment_ids,
    pad_mask,
    segment_image,
    ada_weight,
    ada_bias,
    qkv_weight,
    trunk_bias,
    proj_weight,
    fc1_weight,
    fc2_weight,
    output_grad,
):
    rows, width = tokens.shape
    hidden_width = fc1_weight.shape[1]
    me = lax.axis_index("narrow")
    wide = lax.axis_index("wide")
    stages = n_wide.bit_length() - 1
    low_stages = (n_wide // n_narrow).bit_length() - 1
    hi = wide >> low_stages
    heads = HEADS // n_narrow
    half_heads = heads // 2
    head_width = heads * HEAD
    fc_width = hidden_width // n_narrow
    own_blocks = rows // SMALL
    image_count = conditions.shape[0]
    biases = trunk_bias.astype(F32)
    query_bias = biases[:width]
    value_bias = biases[width : 2 * width]
    proj_bias = biases[2 * width : 3 * width][None, :]
    first_bias = biases[3 * width : 3 * width + hidden_width]
    second_bias = biases[3 * width + hidden_width :][None, :]
    mine_of = functools.partial(lax.dynamic_slice_in_dim, axis=0)

    token_shards = shards_of(tokens, n_narrow)
    labels = gather_relative(segment_ids * 2 + pad_mask, "narrow", n_narrow).reshape(-1)
    grad_shards = shards_of(after(output_grad, token_shards[-1]), n_narrow)

    conditions32 = conditions.astype(F32)
    act = jax.nn.silu(conditions32).astype(BF16)
    columns = (
        jnp.dot(act, ada_weight, preferred_element_type=F32) + ada_bias.astype(F32)
    ).astype(BF16)
    modulation = absolute(gather_relative(columns, "narrow", n_narrow), me, n_narrow)
    modulation = modulation.transpose(1, 0, 2).reshape(image_count, -1)
    slots = labels[::SMALL] >> 1
    image = jnp.sum(
        jnp.where(
            slots[:, None] == jnp.arange(image_count, dtype=jnp.int32)[None, :],
            segment_image[0][None, :],
            0,
        ),
        axis=1,
    )
    pick = image[:, None] == jnp.arange(image_count, dtype=jnp.int32)[None, :]
    per_block = jnp.dot(pick.astype(BF16), modulation, preferred_element_type=F32)[:, None, :]

    qkv_turned = turned_weight(qkv_weight, me, head_width)
    qkv_bias = jnp.concatenate(
        [
            mine_of(query_bias, me * head_width, head_width),
            jnp.zeros((head_width,), F32),
            mine_of(value_bias, me * head_width, head_width),
        ]
    )
    first_in_turned = first_norm(token_shards, per_block)
    tokens_all = jnp.concatenate(token_shards, axis=0)
    projected = (nn(qkv_turned, first_in_turned) + qkv_bias[:, None]).astype(BF16)
    projected = projected.reshape(3, heads, HEAD, -1)
    attended0, log_total0 = attend_forward(projected, labels, 0, half_heads)
    attended1, log_total1 = attend_forward(
        after(projected, attended0), labels, half_heads, half_heads
    )
    half_width = half_heads * HEAD
    attended = [attended0.reshape(half_width, -1), attended1.reshape(half_width, -1)]
    gathered = []
    for part in attended:
        gathered.append(shards_of(part, n_narrow))

    fc1_mine = lax.dynamic_slice_in_dim(fc1_weight, me * fc_width, fc_width, axis=1)
    fc2_mine = lax.dynamic_slice_in_dim(fc2_weight, me * fc_width, fc_width, axis=0)
    output_grad_all = after(jnp.concatenate(grad_shards, axis=0), attended1)
    gate2 = per_block[:, :, 5 * width :]
    branch2_grad_all = flat(gate2 * blocked(output_grad_all.astype(F32))).astype(BF16)
    hidden_grad = nt(branch2_grad_all, fc2_mine).astype(BF16)

    branch1, middle, second_in_all = second_norm(
        [gathered[s][j] for j in range(n_narrow) for s in range(2)],
        me,
        proj_weight,
        proj_bias,
        per_block,
        after(tokens_all, hidden_grad),
        rows,
    )

    hidden, before_grad, before_sums = hidden_and_grad(
        second_in_all,
        fc1_weight,
        fc1_mine,
        mine_of(first_bias, me * fc_width, fc_width)[None, :],
        hidden_grad,
        me,
    )
    own_grad, *other_grads = row_shards(before_grad, rows, 0)
    second_in_others = [nt(g, fc1_mine).astype(BF16) for g in other_grads]
    second_in_mine = nt(after(own_grad, *second_in_others), fc1_mine)
    second_in_parts = [second_in_mine] + received(second_in_others, n_narrow)
    fc2_local = tn(after(hidden, second_in_mine), branch2_grad_all).astype(BF16)
    fc1_local = tn(after(second_in_all, fc2_local), before_grad).astype(BF16)

    fc2_sum = Halving(fc2_local, low_stages, n_wide, wide)
    fc1_sum = Halving(fc1_local, stages, n_wide, wide)
    tied = fc2_sum.step(fc1_local)

    middle_grad, branch1_grad, second_sums = second_back(
        second_in_parts, after(middle, tied), branch1, output_grad, per_block
    )
    branch1_grad_all = jnp.concatenate(shards_of(branch1_grad, n_narrow), axis=0)
    own_hidden, *other_hidden = row_shards(after(hidden, branch1_grad), rows, 0)
    branch2_others = [nn(h, fc2_mine).astype(BF16) for h in other_hidden]
    branch2_mine = nn(own_hidden, fc2_mine)
    tied = fc1_sum.step((branch2_mine, branch2_others))
    branch1_grad_all = after(branch1_grad_all, tied)
    proj_mine = lax.dynamic_slice_in_dim(proj_weight, me * head_width, head_width, axis=0)
    attended_grad = nt(proj_mine, branch1_grad_all).astype(BF16).reshape(heads, HEAD, -1)
    projected_grad0 = attend_backward(projected, attended_grad, attended0, log_total0, labels, 0)
    branch2_parts = [branch2_mine] + received(
        [after(b, branch1_grad_all) for b in branch2_others], n_narrow
    )
    tied = fc2_sum.step(projected_grad0)
    grad0 = projected_grad0.reshape(3 * half_width, -1)
    qkv0_pair = weight_halves(first_in_turned, after(grad0, tied), wide, n_wide)
    qkv0_sum = Halving(None, stages, n_wide, wide, qkv0_pair)
    proj_local = jnp.concatenate(
        [nn(after(a, qkv0_pair[0]), branch1_grad_all).astype(BF16) for a in attended], axis=0
    )
    proj_sum = Halving(proj_local, low_stages, n_wide, wide)
    output, output_sums = finish_output(
        branch2_parts,
        middle,
        after(output_grad, proj_local),
        per_block,
        second_bias,
    )
    tied = fc1_sum.step(output)

    def put(size, part):
        return lax.dynamic_update_slice_in_dim(
            jnp.zeros((size,), F32), part, me * part.shape[0], axis=0
        )

    def put_half(part):
        return put(width, jnp.concatenate([part, jnp.zeros((half_width,), F32)]))

    bias_local = jnp.concatenate(
        [
            put_half(jnp.sum(grad0[:half_width].astype(F32), axis=1)),
            put_half(jnp.sum(grad0[2 * half_width :].astype(F32), axis=1)),
            jnp.sum(second_sums[:, 3], axis=0),
            put(hidden_width, before_sums[0]),
            jnp.sum(output_sums[:, 1], axis=0),
        ]
    )
    bias_width = bias_local.shape[0] // (n_wide * n_narrow)
    bias_local = bias_local.reshape(n_wide, n_narrow, bias_width).transpose(1, 0, 2)
    bias_local = bias_local.reshape(n_narrow, image_count, -1)
    projected_grad1 = attend_backward(
        projected,
        after(attended_grad, tied, proj_sum.step(output), bias_local),
        attended1,
        log_total1,
        labels,
        half_heads,
    )
    grad1 = projected_grad1.reshape(3 * half_width, -1)

    tied = qkv0_sum.step(projected_grad1)
    projected_grad = jnp.concatenate([projected_grad0, projected_grad1], axis=1)
    projected_grad = after(projected_grad.reshape(3 * head_width, -1), tied)
    grad_shards1 = row_shards(projected_grad, rows, 1)
    first_in_others = [tn(g, qkv_turned).astype(BF16) for g in grad_shards1[1:]]
    first_in_arrived = received(first_in_others, n_narrow)
    qkv1_pair = weight_halves(
        first_in_turned, after(grad1, *first_in_others), wide, n_wide
    )
    qkv1_sum = Halving(None, stages, n_wide, wide, qkv1_pair)
    own_grads = after(grad_shards1[0], qkv1_pair[0])
    first_in_mine = tn(own_grads, qkv_turned)
    tied = (qkv1_sum.step(first_in_mine), fc2_sum.step(first_in_mine))

    first_block_sums = first_sums(
        [after(g, tied) for g in [first_in_mine] + first_in_others], token_shards
    )
    tied = qkv0_sum.step(first_block_sums)

    def by_image(choice, sums):
        return lax.dot_general(
            choice.astype(F32),
            sums.reshape(sums.shape[0], -1),
            (((0,), (0,)), ((), ())),
            precision=lax.Precision.HIGHEST,
            preferred_element_type=F32,
        )

    modulation_part = jnp.concatenate(
        [
            by_image(pick, first_block_sums),
            by_image(pick[:own_blocks], second_sums[:, :3]),
            by_image(pick[:own_blocks], output_sums[:, :1]),
        ],
        axis=1,
    )
    modulation_part = modulation_part.reshape(image_count, n_narrow, -1).transpose(1, 0, 2)

    per_row = n_wide // image_count
    shape = (n_narrow, image_count, per_row * bias_width)
    owner = lax.broadcasted_iota(jnp.int32, shape, 0)
    row = lax.broadcasted_iota(jnp.int32, shape, 1)
    column = lax.broadcasted_iota(jnp.int32, shape, 2) // bias_width
    place = (row * per_row + column) * n_narrow + owner
    for first, base in ((0, 0), (2 * half_width, width)):
        sums = jnp.sum(grad1[first : first + half_width].astype(F32), axis=1)
        start = (base + me * head_width + half_width) // bias_width
        for k in range(half_width // bias_width):
            line = jnp.tile(sums[k * bias_width : (k + 1) * bias_width], per_row)
            bias_local = bias_local + jnp.where(place == start + k, line[None, None, :], 0.0)
    small = jnp.concatenate([modulation_part, bias_local], axis=2)
    relative = absolute(small, me, n_narrow)
    small = scatter_relative(
        relative[0], [relative[j] for j in range(1, n_narrow)], "narrow", n_narrow
    ).astype(BF16)
    tokens_grad = first_back(
        [first_in_mine] + first_in_arrived,
        tokens,
        after(middle_grad, relative, qkv0_sum.value),
        per_block,
    )
    column_count = small.shape[1] - n_wide * bias_width // image_count
    modulation_grad = small[:, :column_count]
    together = jnp.concatenate([small, act], axis=1)[None]
    tied = qkv1_sum.step(tokens_grad)
    plan = [
        lambda anchor: (qkv0_sum.step(anchor), proj_sum.step(anchor), fc1_sum.step(anchor)),
        lambda anchor: (qkv1_sum.step(anchor),),
        lambda anchor: (qkv0_sum.step(anchor), proj_sum.step(anchor), fc1_sum.step(anchor)),
        lambda anchor: (qkv1_sum.step(anchor),),
    ]
    for stage in range(stages):
        arrived = swap(together, "wide", n_wide, n_wide >> (stage + 1))
        together = jnp.concatenate([after(together, tied), arrived], axis=0)
        if stage == 1:
            modulation_grad = after(modulation_grad, together)
        if stage < len(plan):
            tied = plan[stage](together)
    qkv0_sum.finish(together)
    qkv1_sum.finish(together)
    fc1_sum.finish(together)
    proj_sum.finish(together)
    bias_sum = jnp.sum(together[:, :, column_count:-width].astype(F32), axis=0)
    bias_sum = lax.dynamic_index_in_dim(
        bias_sum.reshape(n_wide, bias_width), wide, 0, keepdims=False
    )
    together = after(together, qkv1_sum.value).reshape(n_wide * image_count, -1)
    modulation_grad_all = together[:, :column_count]
    ada_weight_grad = tn(together[:, -width:], modulation_grad_all)
    ada_bias_grad = jnp.sum(modulation_grad_all.astype(F32), axis=0)

    proj_flat = rows_to_columns(proj_sum.value, n_wide, n_narrow, hi, ada_weight_grad)
    fc2_flat = rows_to_columns(
        fc2_sum.finish(output), n_wide, n_narrow, hi, together
    )
    fc1_flat = fc1_sum.value.astype(F32)
    qkv_sum = jnp.stack([qkv0_sum.value, qkv1_sum.value]).reshape(2, -1, 3, half_width)
    qkv_all = absolute(gather_relative(qkv_sum, "narrow", n_narrow), me, n_narrow)
    qkv_all = qkv_all.transpose(2, 3, 0, 1, 4).reshape(qkv_sum.shape[1], 3 * width)
    qkv_block = 3 * width // n_narrow
    qkv_flat = lax.dynamic_slice_in_dim(qkv_all, me * qkv_block, qkv_block, axis=1)

    act_part = nt(modulation_grad, ada_weight)
    act_part = act_part.reshape(image_count, n_narrow, -1).transpose(1, 0, 2)
    relative = absolute(act_part, me, n_narrow)
    act_grad = scatter_relative(
        relative[0], [relative[j] for j in range(1, n_narrow)], "narrow", n_narrow
    )
    column_width = width // n_narrow
    condition_mine = lax.dynamic_slice_in_dim(conditions32, me * column_width, column_width, 1)
    gate = 1.0 / (1.0 + jnp.exp(-condition_mine))
    conditions_grad = act_grad * (gate * (1.0 + condition_mine * (1.0 - gate)))

    return (
        output,
        tokens_grad,
        conditions_grad,
        ada_weight_grad,
        ada_bias_grad,
        qkv_flat.astype(F32).reshape(1, -1),
        bias_sum.reshape(-1),
        proj_flat.reshape(1, -1),
        fc1_flat.reshape(1, -1),
        fc2_flat.reshape(1, -1),
    )


def solution(mesh):
    placed = (
        P(("wide", "narrow"), None),
        P("wide", None),
        P(("wide", "narrow")),
        P(("wide", "narrow")),
        P("wide", None),
        P(None, "narrow"),
        P("narrow"),
        P(),
        P(),
        P(),
        P(),
        P(),
        P(("wide", "narrow"), None),
    )
    return jax.shard_map(
        functools.partial(body, mesh.shape["wide"], mesh.shape["narrow"]),
        mesh=mesh,
        in_specs=placed,
        out_specs=(
            P(("wide", "narrow"), None),
            P(("wide", "narrow"), None),
            P("wide", "narrow"),
            P(None, "narrow"),
            P("narrow"),
            P("narrow", "wide"),
            P(("wide", "narrow")),
            P("narrow", "wide"),
            P("narrow", "wide"),
            P("narrow", "wide"),
        ),
        check_vma=False,
    )
```
